32 devices in a mesh: mem: 4 (over x, core), lat: 8 (over z, y).
Axes of the slice: x: 2, y: 2, z: 4, core: 2. Of those that a mesh axis runs over, the one named last changes fastest.
Arguments:
- perturb: bfloat16 [64, 3, 5, 64, 1440], P('mem', None, None, 'lat'), may hold values from -0.75 to 0.75
- innovation: float32 [3, 5, 64, 1440], P(None, None, 'lat'), may hold values from -6 to 6
- obs_weight: float32 [3, 5, 64, 1440], P(None, None, 'lat'), may hold values from 0.3 to 3
- lon_coef: float32 [64, 1440], P('lat'), may hold values from 0.03 to 0.12
- lat_coef: float32 [64, 1440], P('lat'), may hold values from 0.03 to 0.12
Outputs:
- control: float32 [64, 64, 1440], P('mem', 'lat')
- increment: float32 [3, 5, 64, 1440], P(None, None, 'lat')
The draws below stay inside these ranges and needn't reach their ends.
All inputs are finite; a program needn't handle non-finite values.
Results may differ from the reference program's by a relative error of at most 0.0003.
Values sent between devices are 32-bit elements; how exact they have to be, the bound alone decides.
No kernel may reach another device: no remote copies, remote signals or barrier semaphores. Data moves between devices by JAX's collectives and lax.ppermute only.
A program may use at most 128 MiB of HBM per device.

```python
import math
import jax
import jax.numpy as jnp
from jax import lax

MEMBERS = 64
SLOTS = 3
VARS = 5
NLON = 1440
NLAT = 64
PASSES = 10
ITERS = 2


def levels(rng, dims, cuts, low, largest):
    def one(dim, parts):
        steps = jax.random.uniform(jax.random.fold_in(jax.random.fold_in(rng, 6), dim), (parts,), jnp.float32, low / len(cuts), largest / len(cuts))
        return jnp.repeat(jnp.exp(steps), dims[dim] // parts).reshape((-1,) + (1,) * (len(dims) - dim - 1))

    loudness = one(*cuts[0])
    for cut in cuts[1:]:
        loudness = loudness * one(*cut)
    return loudness


def normal_values(stream_key, extent, deviation, limit, split=(), kind=jnp.bfloat16):
    gain = levels(stream_key, extent, split, -0.22, 0.18) if split else 1.0
    entries = jax.random.normal(stream_key, extent, jnp.float32) * deviation * gain
    return jnp.minimum(jnp.maximum(entries, -limit), limit).astype(kind)


def setup_inputs(seed: int = 0) -> dict:
    streams_of = jax.random.split(jax.random.key(seed), 6)
    perturb = normal_values(streams_of[0], (MEMBERS, SLOTS, VARS, NLAT, NLON), MEMBERS ** -0.5, 0.75, ((0, 4), (3, 8)))
    innovation = normal_values(streams_of[1], (SLOTS, VARS, NLAT, NLON), 1.0, 6.0, ((2, 8),), jnp.float32)
    obs_weight = jnp.clip(jnp.exp(math.log(3.0) - 2.3025851 * jax.random.uniform(streams_of[2], (SLOTS, VARS, NLAT, NLON), jnp.float32) ** levels(streams_of[2], (SLOTS, VARS, NLAT, NLON), ((2, 8),), -0.2, 0.2)), 0.3, 3.0)
    lon_coef = jnp.clip(jnp.exp(math.log(0.12) - 1.3862944 * jax.random.uniform(streams_of[3], (NLAT, NLON), jnp.float32) ** levels(streams_of[3], (NLAT, NLON), ((0, 8),), -0.2, 0.2)), 0.03, 0.12)
    lat_coef = jnp.clip(jnp.exp(math.log(0.12) - 1.3862944 * jax.random.uniform(streams_of[4], (NLAT, NLON), jnp.float32) ** levels(streams_of[4], (NLAT, NLON), ((0, 8),), -0.2, 0.2)), 0.03, 0.12)
    return dict(perturb=perturb, innovation=innovation, obs_weight=obs_weight, lon_coef=lon_coef, lat_coef=lat_coef)


def diffuse(values, lon_coef, lat_coef):
    zeros_row = jnp.zeros_like(values[:, :1])
    lat_upper = jnp.concatenate([lat_coef[1:], jnp.zeros_like(lat_coef[:1])], 0)
    lon_western = jnp.roll(lon_coef, 1, axis=1)
    for repeat in range(PASSES):
        northward = jnp.concatenate([values[:, 1:], zeros_row], 1)
        southern = jnp.concatenate([zeros_row, values[:, :-1]], 1)
        eastern = jnp.roll(values, -1, axis=2)
        western = jnp.roll(values, 1, axis=2)
        values = (values + lat_upper * (northward - values) - lat_coef * (values - southern)
                  + lon_coef * (eastern - values) - lon_western * (values - western))
    return values


def ensemble_map(perturb, fields):
    def add_member(total, pair):
        member_pert, member_field = pair
        return total + member_pert.astype(jnp.float32) * member_field, None
    start = jnp.zeros(perturb.shape[1:], jnp.float32)
    total, unused = lax.scan(add_member, start, (perturb, fields))
    return total


def ensemble_adjoint(perturb, weighted):
    def one_member(member_pert):
        return jnp.sum(member_pert.astype(jnp.float32) * weighted, axis=(0, 1))
    return lax.map(one_member, perturb)


def reference(perturb, innovation, obs_weight, lon_coef, lat_coef):
    def hessian(direction):
        smoothed = diffuse(direction, lon_coef, lat_coef)
        weighted = obs_weight * ensemble_map(perturb, smoothed)
        return direction + diffuse(ensemble_adjoint(perturb, weighted), lon_coef, lat_coef)

    right_side = diffuse(ensemble_adjoint(perturb, obs_weight * innovation), lon_coef, lat_coef)
    control = jnp.zeros_like(right_side)
    residual = right_side
    direction = right_side
    norm_now = jnp.sum(residual * residual)
    for count in range(ITERS):
        image = hessian(direction)
        step_size = norm_now / jnp.sum(direction * image)
        control = control + step_size * direction
        residual = residual - step_size * image
        norm_next = jnp.sum(residual * residual)
        direction = residual + (norm_next / norm_now) * direction
        norm_now = norm_next
    increment = ensemble_map(perturb, diffuse(control, lon_coef, lat_coef))
    return control, increment
```

```python
import functools

import jax
import jax.numpy as jnp
from jax import lax
from jax.experimental import pallas as pl
from jax.experimental.pallas import tpu as pltpu
from jax.sharding import PartitionSpec as P

PASSES = 10
LANES = 128
SUB = 8


def ceil_to(value, unit):
    return -(-value // unit) * unit


class Plan:
    def __init__(self, perturb, lat_coef, mem, lat):
        self.members, self.slots, self.vars, self.rows, self.nlon = perturb.shape
        self.mem, self.lat = mem, lat
        self.fields = self.slots * self.vars
        self.half = (self.fields + 2) // 2
        self.wide = ceil_to(self.nlon + 16, LANES)
        halo = -(-2 * PASSES // self.rows)
        self.group = max(
            g for g in range(1, lat + 1)
            if lat % g == 0 and self.members % g == 0 and (g == lat or g >= halo)
        )
        self.groups = lat // self.group
        self.halo = 0 if self.groups == 1 else halo
        self.share = self.members // self.group
        self.window = self.group + 2 * self.halo
        self.run = self.window * self.rows
        self.used = self.share * self.run
        self.lanes = ceil_to(self.used, LANES)
        self.tiles = self.lanes // LANES
        self.step = self.nlon // SUB
        self.unroll = max(u for u in range(1, 21) if self.step % u == 0)


def adjoint_kernel(p, second, *refs):
    if second:
        perturb, weight, mine, other, out, total, scal, prod, full = refs
    else:
        perturb, weight, value, lon, lat, out, prod = refs
    step = pl.program_id(0)

    if second:
        @pl.when(step == 0)
        def _():
            core = lax.axis_index("mem") % 2
            for k in range(p.half):
                full[core * p.half + k] = mine[k]
                full[(1 - core) * p.half + k] = other[k]
            acc = jnp.zeros((p.rows, p.nlon), jnp.float32)
            for k in range(p.fields):
                t = full[k]
                wt = weight[k] * t
                prod[k] = wt
                total[k] = t
                acc = acc + wt * t
            scal[0] = full[2 * p.half - 1][:, :LANES]
            scal[1] = jnp.full((p.rows, LANES), jnp.sum(acc))
    else:
        @pl.when(step == 0)
        def _():
            for k in range(p.fields):
                prod[k] = weight[k] * value[k]

    for m in range(p.share):
        acc = perturb[m, 0].astype(jnp.float32) * prod[0]
        for k in range(1, p.fields):
            acc = acc + perturb[m, k].astype(jnp.float32) * prod[k]
        out[0, m, :, : p.nlon] = acc
    if second:
        tail = jnp.broadcast_to(scal[1][:1, :1], (p.rows, p.wide - p.nlon))
        for m in range(p.share):
            out[0, m, :, p.nlon :] = tail
    else:
        for m in range(p.share):
            out[0, m, :, p.nlon :] = jnp.zeros((p.rows, p.wide - p.nlon), jnp.float32)
        out[0, p.share, :, : p.nlon] = lon[...]
        out[0, p.share + 1, :, : p.nlon] = lat[...]
        out[0, p.share, :, p.nlon :] = jnp.zeros((p.rows, p.wide - p.nlon), jnp.float32)
        out[0, p.share + 1, :, p.nlon :] = jnp.zeros((p.rows, p.wide - p.nlon), jnp.float32)


def adjoint(p, perturb, weight, *rest, second):
    whole = lambda *shape: pl.BlockSpec(shape, lambda i: (0,) * len(shape))
    rows, nlon = p.rows, p.nlon
    planes = p.share if second else p.share + 2
    field = whole(p.fields, rows, nlon)
    if second:
        more = [whole(p.half, rows, nlon)] * 2
    else:
        more = [field, whole(rows, nlon), whole(rows, nlon)]
    out_shape = [jax.ShapeDtypeStruct((p.group, planes, rows, p.wide), jnp.float32)]
    out_specs = [pl.BlockSpec((1, planes, rows, p.wide), lambda i: (i, 0, 0, 0))]
    scratch = [pltpu.VMEM((p.fields, rows, nlon), jnp.float32)]
    if second:
        out_shape += [
            jax.ShapeDtypeStruct((p.fields, rows, nlon), jnp.float32),
            jax.ShapeDtypeStruct((2, rows, LANES), jnp.float32),
        ]
        out_specs += [field, whole(2, rows, LANES)]
        scratch += [pltpu.VMEM((2 * p.half, rows, nlon), jnp.float32)]
    return pl.pallas_call(
        functools.partial(adjoint_kernel, p, second),
        grid=(p.group,),
        in_specs=[
            pl.BlockSpec((p.share, p.fields, rows, nlon), lambda i: (i, 0, 0, 0)),
            field,
            *more,
        ],
        out_specs=out_specs,
        out_shape=out_shape,
        scratch_shapes=scratch,
        name="adjoint_second" if second else "adjoint_first",
    )(perturb, weight, *rest)


def forward_kernel(p, perturb, field, keep, send, scr):
    step = pl.program_id(0)
    for v in range(p.vars):
        acc = perturb[0, 0, v].astype(jnp.float32) * field[0, :, : p.nlon]
        for m in range(1, p.members):
            acc = acc + perturb[m, 0, v].astype(jnp.float32) * field[m, :, : p.nlon]
        scr[step * p.vars + v] = acc

    @pl.when(step == p.slots - 1)
    def _():
        core = lax.axis_index("mem") % 2
        one = jnp.zeros((1, 1), jnp.float32)
        two = jnp.zeros((1, 1), jnp.float32)
        for k in range(p.group):
            one = one + field[k * p.share, :1, p.nlon : p.nlon + 1]
            two = two + field[k * p.share, :1, p.nlon + SUB : p.nlon + SUB + 1]
        for k in range(p.fields, 2 * p.half):
            scr[k] = jnp.zeros((p.rows, p.nlon), jnp.float32)
        scr[2 * p.half - 1, :, :LANES] = jnp.broadcast_to(one, (p.rows, LANES))
        scr[2 * p.half - 1, :, LANES : 2 * LANES] = jnp.broadcast_to(two, (p.rows, LANES))
        for k in range(p.half):
            keep[k] = scr[core * p.half + k]
            send[k] = scr[(1 - core) * p.half + k]


def forward(p, perturb, field):
    rows, nlon = p.rows, p.nlon
    shape = (p.half, rows, nlon)
    spec = pl.BlockSpec(shape, lambda i: (0, 0, 0))
    return pl.pallas_call(
        functools.partial(forward_kernel, p),
        grid=(p.slots,),
        in_specs=[
            pl.BlockSpec((p.members, 1, p.vars, rows, nlon), lambda i: (0, i, 0, 0, 0)),
            pl.BlockSpec((p.members, rows, p.wide), lambda i: (0, 0, 0)),
        ],
        out_specs=[spec, spec],
        out_shape=[jax.ShapeDtypeStruct(shape, jnp.float32)] * 2,
        scratch_shapes=[pltpu.VMEM((2 * p.half, rows, nlon), jnp.float32)],
        name="forward",
    )(perturb, field)


def roll(x, shift, axis):
    return pltpu.roll(x, shift % x.shape[axis], axis)


def flip(p, pick, sheet):
    for j in range(p.wide // LANES):
        cols = slice(j * LANES, (j + 1) * LANES)
        tiles = [pick(c, m, cols) for m in range(p.share) for c in range(p.window)]
        if p.used < p.lanes:
            tiles.append(jnp.zeros((p.lanes - p.used, LANES), jnp.float32))
        block = jnp.concatenate(tiles, axis=0)
        for t in range(p.tiles):
            sheet[t, cols, :] = block[t * LANES : (t + 1) * LANES].T


def unflip(p, sheet, out, stop):
    for j in range(-(-stop // LANES)):
        low, high = j * LANES, min((j + 1) * LANES, stop)
        block = [sheet[t, low : low + LANES, :].T for t in range(p.tiles)]
        for m in range(p.share):
            for c in range(p.group):
                at = m * p.run + (p.halo + c) * p.rows
                piece = block[at // LANES][at % LANES : at % LANES + p.rows]
                out[c, m, :, low:high] = piece[:, : high - low]


def lane_row(p):
    lane = lax.broadcasted_iota(jnp.int32, (SUB, p.lanes), 1)
    return lane % p.run, lane


def wrap(p, buf):
    buf[0] = roll(buf[p.step], 1, 0)
    buf[p.step + 1] = roll(buf[1], -1, 0)


def tile(t):
    return slice(t * LANES, (t + 1) * LANES)


def sheet_to(p, sheet, buf):
    def one(i, none):
        for t in range(p.tiles):
            buf[i + 1, :, tile(t)] = sheet[t, pl.ds(i, SUB, stride=p.step), :]
        return none
    lax.fori_loop(0, p.step, one, 0, unroll=p.unroll)


def to_sheet(p, buf, sheet):
    def one(i, none):
        for t in range(p.tiles):
            sheet[t, pl.ds(i, SUB, stride=p.step), :] = buf[i + 1, :, tile(t)]
        return none
    lax.fori_loop(0, p.step, one, 0, unroll=p.unroll)


def one_pass(p, src, dst, east, north, diag):
    def body(c, carry):
        f, west = carry
        for k in range(p.unroll):
            i = 1 + c * p.unroll + k
            fe = src[i + 1]
            flux = east[i] * (fe - f)
            up = north[i] * (roll(f, -1, 1) - f)
            dst[i] = diag[i] * f + ((up - roll(up, 1, 1)) + (flux - west))
            f, west = fe, flux
        return f, west
    f = src[1]
    lax.fori_loop(0, p.step // p.unroll, body, (f, east[0] * (f - src[0])))
    wrap(p, dst)


def ten(p, a, b, east, north, diag):
    def two(_, none):
        one_pass(p, a, b, east, north, diag)
        one_pass(p, b, a, east, north, diag)
        return none
    lax.fori_loop(0, PASSES // 2, two, 0)
    if PASSES % 2:
        one_pass(p, a, b, east, north, diag)
        a[...] = b[...]


def total_of(p, own, term):
    def one(i, acc):
        return acc + term(i + 1)
    acc = lax.fori_loop(0, p.step, one, jnp.zeros((SUB, p.lanes), jnp.float32), unroll=p.unroll)
    return jnp.sum(jnp.where(own, acc, 0.0))


def own_lanes(p):
    row, lane = lane_row(p)
    first = p.halo * p.rows
    return (row >= first) & (row < first + p.group * p.rows) & (lane < p.used)


def first_kernel(p, got, out, right, east, north, diag, sheet, a, b):
    row, lane = lane_row(p)
    low = 0
    high = p.run - 1
    if p.groups > 1:
        here = lax.axis_index("lat") // p.group * p.group - p.halo
        low = jnp.maximum(-here, 0) * p.rows
        high = jnp.minimum(p.lat - here, p.window) * p.rows - 1
    flip(p, lambda c, m, cols: got[c, p.share + 1, :, cols], sheet)
    sheet_to(p, sheet, a)
    inside = (row >= low) & (row <= high) & (lane < p.used)

    def coefs(i, none):
        here = jnp.where(inside, a[i + 1], 0.0)
        north[i + 1] = jnp.where(inside & (row < high), roll(here, -1, 1), 0.0)
        diag[i + 1] = 1.0 - jnp.where(row == low, here, 0.0)
        return none
    lax.fori_loop(0, p.step, coefs, 0, unroll=p.unroll)
    flip(p, lambda c, m, cols: got[c, p.share, :, cols], sheet)
    sheet_to(p, sheet, east)
    wrap(p, east)
    flip(p, lambda c, m, cols: got[c, m, :, cols], sheet)
    sheet_to(p, sheet, a)
    wrap(p, a)
    ten(p, a, b, east, north, diag)

    def keep(i, none):
        right[i + 1] = a[i + 1]
        return none
    lax.fori_loop(0, p.step, keep, 0, unroll=p.unroll)
    rr = total_of(p, own_lanes(p), lambda i: right[i] * right[i])
    ten(p, a, b, east, north, diag)
    to_sheet(p, a, sheet)
    sheet[:, p.nlon :, :] = jnp.full((p.tiles, p.wide - p.nlon, LANES), rr)
    unflip(p, sheet, out, p.wide)


def second_kernel(p, got, right, east, north, diag, scal, out, resid, ahead, sheet, a, b):
    row, lane = lane_row(p)
    flip(p, lambda c, m, cols: got[c, m, :, cols], sheet)
    if p.groups == 1:
        q = 0.0
        for t in range(p.tiles):
            first = (row[:1, tile(t)] % p.rows == 0) & (lane[:1, tile(t)] < p.run)
            q = q + jnp.sum(jnp.where(first, sheet[t, p.nlon : p.nlon + 1, :], 0.0))
        q = jnp.full((SUB, LANES), q)
    else:
        q = scal[1][:SUB]
    rr = scal[0][:SUB]
    alpha = rr / (rr + q)
    ahead[...] = alpha
    sheet_to(p, sheet, a)
    wrap(p, a)
    ten(p, a, b, east, north, diag)
    alpha = jnp.broadcast_to(alpha[:, :1], (SUB, p.lanes))

    def cut(i, none):
        r = right[i + 1]
        r = r - alpha * (r + a[i + 1])
        a[i + 1] = r
        resid[i + 1] = r
        return none
    lax.fori_loop(0, p.step, cut, 0, unroll=p.unroll)
    wrap(p, a)
    own = own_lanes(p)
    rr1 = total_of(p, own, lambda i: resid[i] * resid[i])
    rb = total_of(p, own, lambda i: resid[i] * right[i])
    ten(p, a, b, east, north, diag)
    to_sheet(p, a, sheet)
    sheet[:, p.nlon :, :] = jnp.zeros((p.tiles, p.wide - p.nlon, LANES), jnp.float32)
    sheet[:, p.nlon : p.nlon + SUB, :] = jnp.full((p.tiles, SUB, LANES), rr1)
    sheet[:, p.nlon + SUB : p.nlon + 2 * SUB, :] = jnp.full((p.tiles, SUB, LANES), rb)
    unflip(p, sheet, out, p.wide)


def buffers(p):
    buf = (p.step + 2, SUB, p.lanes)
    return [pltpu.VMEM((p.tiles, p.wide, LANES), jnp.float32)] + [pltpu.VMEM(buf, jnp.float32)] * 2


def vmem(n):
    return [pl.BlockSpec(memory_space=pltpu.VMEM)] * n


def first_half(p, got):
    buf = jax.ShapeDtypeStruct((p.step + 2, SUB, p.lanes), jnp.float32)
    back = jax.ShapeDtypeStruct((p.group, p.share, p.rows, p.wide), jnp.float32)
    return pl.pallas_call(
        functools.partial(first_kernel, p),
        in_specs=vmem(1),
        out_specs=vmem(5),
        out_shape=[back, buf, buf, buf, buf],
        scratch_shapes=buffers(p),
        name="smooth_first",
    )(got)


def second_half(p, got, right, east, north, diag, scal):
    buf = jax.ShapeDtypeStruct((p.step + 2, SUB, p.lanes), jnp.float32)
    back = jax.ShapeDtypeStruct((p.group, p.share, p.rows, p.wide), jnp.float32)
    return pl.pallas_call(
        functools.partial(second_kernel, p),
        in_specs=vmem(6),
        out_specs=vmem(3),
        out_shape=[back, buf, jax.ShapeDtypeStruct((SUB, LANES), jnp.float32)],
        scratch_shapes=buffers(p),
        name="smooth_second",
    )(got, right, east, north, diag, scal)


def test_kernel(p, weight, total, mine, other, scal, both, sums, part, full):
    core = lax.axis_index("mem") % 2
    for k in range(p.half):
        full[core * p.half + k] = mine[k]
        full[(1 - core) * p.half + k] = other[k]
    rr1 = full[2 * p.half - 1][:, :LANES]
    rb = full[2 * p.half - 1][:, LANES : 2 * LANES]
    rr = scal[0]
    beta = rr1 / rr
    acc = jnp.zeros((p.rows, p.nlon), jnp.float32)
    for k in range(p.fields):
        t = full[k] + beta[:1, :1] * total[k]
        both[k] = t
        acc = acc + weight[k] * t * t
    sums[0] = rr1
    sums[1] = beta
    sums[2] = rr1 + beta * (2.0 * rb + beta * rr)
    part[...] = jnp.full((p.rows, LANES), jnp.sum(acc))


def test(p, weight, total, mine, other, scal):
    return pl.pallas_call(
        functools.partial(test_kernel, p),
        in_specs=vmem(5),
        out_specs=vmem(3),
        out_shape=[
            jax.ShapeDtypeStruct((p.fields, p.rows, p.nlon), jnp.float32),
            jax.ShapeDtypeStruct((3, p.rows, LANES), jnp.float32),
            jax.ShapeDtypeStruct((p.rows, LANES), jnp.float32),
        ],
        scratch_shapes=[pltpu.VMEM((2 * p.half, p.rows, p.nlon), jnp.float32)],
        name="last_sums",
    )(weight, total, mine, other, scal)


def last_kernel(p, total, both, sums, ahead, q, right, resid, grown, back, sheet):
    step2 = sums[0] / (sums[2] + q[...])
    step1 = ahead[: p.rows]
    for k in range(p.fields):
        grown[k] = step1[:1, :1] * total[k] + step2[:1, :1] * both[k]
    near = step1 + step2 * sums[1]
    near = jnp.broadcast_to(near[:1, :1], (SUB, LANES))
    far = jnp.broadcast_to(step2[:1, :1], (SUB, LANES))

    def one(i, none):
        for t in range(p.tiles):
            at = (i + 1, slice(None), tile(t))
            sheet[t, pl.ds(i, SUB, stride=p.step), :] = near * right[at] + far * resid[at]
        return none
    lax.fori_loop(0, p.step, one, 0, unroll=p.unroll)
    sheet[:, p.nlon :, :] = jnp.zeros((p.tiles, p.wide - p.nlon, LANES), jnp.float32)
    unflip(p, sheet, back, p.nlon)


def last(p, total, both, sums, ahead, q, right, resid):
    return pl.pallas_call(
        functools.partial(last_kernel, p),
        in_specs=vmem(7),
        out_specs=vmem(2),
        out_shape=[
            jax.ShapeDtypeStruct((p.fields, p.rows, p.nlon), jnp.float32),
            jax.ShapeDtypeStruct((p.group, p.share, p.rows, p.nlon), jnp.float32),
        ],
        scratch_shapes=[pltpu.VMEM((p.tiles, p.wide, LANES), jnp.float32)],
        name="last_update",
    )(total, both, sums, ahead, q, right, resid)


def swap(p, x, axis, bit, count):
    return lax.ppermute(x, axis, [(i, i ^ bit) for i in range(count)])


def turn(p, x):
    if p.groups == 1:
        return lax.all_to_all(x, "lat", 0, 0)
    sets = [[g * p.group + i for i in range(p.group)] for g in range(p.groups)]
    return lax.all_to_all(x, "lat", 0, 0, axis_index_groups=sets)


def widen(p, x):
    if p.groups == 1:
        return x
    gap = p.group
    up = [(i, i + gap) for i in range(p.lat - gap)]
    down = [(i + gap, i) for i in range(p.lat - gap)]
    before = lax.ppermute(x[-p.halo :], "lat", up)
    after = lax.ppermute(x[: p.halo], "lat", down)
    return jnp.concatenate([before, x, after], axis=0)


def member_sum(p, keep, send):
    mine = keep + swap(p, send, "mem", 1, p.mem)
    bit = 2
    while bit < p.mem:
        mine = mine + swap(p, mine, "mem", bit, p.mem)
        bit *= 2
    other = swap(p, mine, "mem", 1, p.mem)
    if p.groups > 1:
        mine, other = (regroup(p, x) for x in (mine, other))
    return mine, other


def regroup(p, x):
    sums = lax.psum(x[-1:], "lat") / p.group
    return jnp.concatenate([x[:-1], sums], axis=0)


def lat_sum(p, x):
    bit = 1
    while bit < p.lat:
        x = x + swap(p, x, "lat", bit, p.lat)
        bit *= 2
    return x


def per_device(perturb, innovation, obs_weight, lon_coef, lat_coef):
    p = Plan(perturb, lat_coef, lax.axis_size("mem"), lax.axis_size("lat"))
    flat = lambda x: x.reshape(p.fields, p.rows, p.nlon)
    weight = flat(obs_weight)
    by_member = perturb.reshape(p.members, p.fields, p.rows, p.nlon)

    (sent,) = adjoint(p, by_member, weight, flat(innovation), lon_coef, lat_coef, second=False)
    back, right, east, north, diag = first_half(p, widen(p, turn(p, sent)))
    field = turn(p, back).reshape(p.members, p.rows, p.wide)
    mine, other = member_sum(p, *forward(p, perturb, field))
    sent, total, scal = adjoint(p, by_member, weight, mine, other, second=True)
    if p.groups > 1:
        scal = jnp.concatenate([scal[:1], lax.psum(scal[1:], "lat")], axis=0)
    back, resid, ahead = second_half(p, widen(p, turn(p, sent)), right, east, north, diag, scal)
    field = turn(p, back).reshape(p.members, p.rows, p.wide)
    mine, other = member_sum(p, *forward(p, perturb, field))
    both, sums, part = test(p, weight, total, mine, other, scal)
    grown, back = last(p, total, both, sums, ahead, lat_sum(p, part), right, resid)
    control = turn(p, back).reshape(p.members, p.rows, p.nlon)
    return control, grown.reshape(p.slots, p.vars, p.rows, p.nlon)


def solution(mesh):
    return jax.shard_map(
        per_device,
        mesh=mesh,
        in_specs=(
            P("mem", None, None, "lat", None),
            P(None, None, "lat", None),
            P(None, None, "lat", None),
            P("lat", None),
            P("lat", None),
        ),
        out_specs=(P("mem", "lat", None), P(None, None, "lat", None)),
        check_vma=False,
    )
```

```python
import functools

import jax
import jax.numpy as jnp
from jax import lax
from jax.experimental import pallas as pl
from jax.experimental.pallas import tpu as pltpu
from jax.sharding import PartitionSpec as P

PASSES = 10
LANES = 128
SUB = 8
ROOM = pltpu.CompilerParams(vmem_limit_bytes=24 * 2**20)


def ceil_to(value, unit):
    return -(-value // unit) * unit


class Plan:
    def __init__(self, perturb, lat_coef, mem, lat):
        self.members, self.slots, self.vars, self.rows, self.nlon = perturb.shape
        self.mem, self.lat = mem, lat
        self.fields = self.slots * self.vars
        self.half = (self.fields + 2) // 2
        self.wide = ceil_to(self.nlon + 16, LANES)
        halo = -(-2 * PASSES // self.rows)
        self.group = max(
            g for g in range(1, lat + 1)
            if lat % g == 0 and self.members % g == 0 and (g == lat or g >= halo)
        )
        self.groups = lat // self.group
        self.halo = 0 if self.groups == 1 else halo
        self.share = self.members // self.group
        self.window = self.group + 2 * self.halo
        self.run = self.window * self.rows
        self.used = self.share * self.run
        self.lanes = ceil_to(self.used, LANES)
        self.tiles = self.lanes // LANES
        self.step = self.nlon // SUB
        self.unroll = max(u for u in range(1, 21) if self.step % u == 0)
        self.stride = max(u for u in range(1, 91) if self.step % u == 0)
        self.parts = max(
            q for q in (1, 2, 4) if mem % q == 0 and self.wide % (q * LANES) == 0
        )
        self.piece = self.wide // self.parts


def adjoint_kernel(p, second, *refs):
    if second:
        perturb, weight, mine, other, out, total, scal, prod = refs
    else:
        perturb, weight, value, out, prod = refs
    step = pl.program_id(0)

    @pl.when(step == 0)
    def _():
        if second:
            core = lax.axis_index("mem") % 2
            acc = jnp.zeros((p.rows, p.nlon), jnp.float32)
            for half, at in ((mine, core * p.half), (other, (1 - core) * p.half)):
                for k in range(p.half):
                    t = half[k, :, : p.nlon]
                    wt = weight[jnp.minimum(at + k, p.fields - 1)] * t
                    prod[at + k] = wt
                    total[at + k] = t
                    acc = acc + wt * t
            rr = mine[0, :1, p.nlon : p.nlon + 1]
            scal[0] = jnp.broadcast_to(rr, (p.rows, LANES))
            scal[1] = jnp.full((p.rows, LANES), jnp.sum(acc))
        else:
            for k in range(p.fields):
                prod[k] = weight[k] * value[k]

    acc = [0.0] * p.share
    for k in range(p.fields):
        row = prod[k]
        for m in range(p.share):
            acc[m] = acc[m] + perturb[m, k].astype(jnp.float32) * row
    tail = jnp.zeros((p.rows, p.wide - p.nlon), jnp.float32)
    if second:
        tail = jnp.broadcast_to(scal[1][:1, :1], tail.shape)
    for m in range(p.share):
        out[0, m, :, : p.nlon] = acc[m]
        out[0, m, :, p.nlon :] = tail


def adjoint(p, perturb, weight, *rest, second):
    whole = lambda *shape: pl.BlockSpec(shape, lambda i: (0,) * len(shape))
    rows, nlon = p.rows, p.nlon
    field = whole(p.fields, rows, nlon)
    more = [whole(p.half, rows, p.wide)] * 2 if second else [field]
    out_shape = [jax.ShapeDtypeStruct((p.group, p.share, rows, p.wide), jnp.float32)]
    out_specs = [pl.BlockSpec((1, p.share, rows, p.wide), lambda i: (i, 0, 0, 0))]
    if second:
        out_shape += [
            jax.ShapeDtypeStruct((2 * p.half, rows, nlon), jnp.float32),
            jax.ShapeDtypeStruct((2, rows, LANES), jnp.float32),
        ]
        out_specs += [whole(2 * p.half, rows, nlon), whole(2, rows, LANES)]
    return pl.pallas_call(
        functools.partial(adjoint_kernel, p, second),
        grid=(p.group,),
        in_specs=[
            pl.BlockSpec((p.share, p.fields, rows, nlon), lambda i: (i, 0, 0, 0)),
            field,
            *more,
        ],
        out_specs=out_specs,
        out_shape=out_shape,
        scratch_shapes=[pltpu.VMEM((2 * p.half, rows, nlon), jnp.float32)],
        cost_estimate=cost(p, 2),
        compiler_params=ROOM,
        name="adjoint_second" if second else "adjoint_first",
    )(perturb, weight, *rest)


def cost(p, size):
    cells = p.members * p.fields * p.rows * p.nlon
    return pl.CostEstimate(flops=2 * cells, bytes_accessed=size * cells, transcendentals=0)


def forward_kernel(p, perturb, field, keep, send, scr):
    step = pl.program_id(0)

    @pl.when(step == 0)
    def _():
        for k in range(2 * p.half):
            scr[k, :, p.nlon :] = jnp.zeros((p.rows, p.wide - p.nlon), jnp.float32)
        for k in range(p.fields, 2 * p.half):
            scr[k, :, : p.nlon] = jnp.zeros((p.rows, p.nlon), jnp.float32)

    split = p.nlon // (2 * LANES) * LANES
    for cols in (slice(0, split), slice(split, p.nlon)):
        acc = [0.0] * p.vars
        for m in range(p.members):
            f = field[m, :, cols]
            for v in range(p.vars):
                acc[v] = acc[v] + perturb[m, 0, v, :, cols].astype(jnp.float32) * f
        for v in range(p.vars):
            scr[step * p.vars + v, :, cols] = acc[v]

    @pl.when(step == p.slots - 1)
    def _():
        core = lax.axis_index("mem") % 2
        one = jnp.zeros((1, 1), jnp.float32)
        two = jnp.zeros((1, 1), jnp.float32)
        for k in range(p.group):
            one = one + field[k * p.share, :1, p.nlon : p.nlon + 1]
            two = two + field[k * p.share, :1, p.nlon + SUB : p.nlon + SUB + 1]
        for k in (0, p.half):
            scr[k, :, p.nlon : p.nlon + SUB] = jnp.broadcast_to(one, (p.rows, SUB))
            scr[k, :, p.nlon + SUB : p.nlon + 2 * SUB] = jnp.broadcast_to(two, (p.rows, SUB))
        for k in range(p.half):
            keep[k] = scr[core * p.half + k]
            send[k] = scr[(1 - core) * p.half + k]


def forward(p, perturb, field):
    rows, nlon = p.rows, p.nlon
    shape = (p.half, rows, p.wide)
    spec = pl.BlockSpec(shape, lambda i: (0, 0, 0))
    return pl.pallas_call(
        functools.partial(forward_kernel, p),
        grid=(p.slots,),
        in_specs=[
            pl.BlockSpec((p.members, 1, p.vars, rows, nlon), lambda i: (0, i, 0, 0, 0)),
            pl.BlockSpec((p.members, rows, p.wide), lambda i: (0, 0, 0)),
        ],
        out_specs=[spec, spec],
        out_shape=[jax.ShapeDtypeStruct(shape, jnp.float32)] * 2,
        scratch_shapes=[pltpu.VMEM((2 * p.half, rows, p.wide), jnp.float32)],
        cost_estimate=cost(p, 2),
        compiler_params=ROOM,
        name="forward",
    )(perturb, field)


def roll(x, shift, axis):
    return pltpu.roll(x, shift % x.shape[axis], axis)


def flip(p, pick, sheet):
    for j in range(p.wide // LANES):
        cols = slice(j * LANES, (j + 1) * LANES)
        tiles = [pick(c, m, cols) for m in range(p.share) for c in range(p.window)]
        if p.used < p.lanes:
            tiles.append(jnp.zeros((p.lanes - p.used, LANES), jnp.float32))
        block = jnp.concatenate(tiles, axis=0)
        for t in range(p.tiles):
            sheet[t, cols, :] = block[t * LANES : (t + 1) * LANES].T


def unflip(p, sheet, out, stop):
    for j in range(-(-stop // LANES)):
        low, high = j * LANES, min((j + 1) * LANES, stop)
        block = [sheet[t, low : low + LANES, :].T for t in range(p.tiles)]
        for m in range(p.share):
            for c in range(p.group):
                at = m * p.run + (p.halo + c) * p.rows
                piece = block[at // LANES][at % LANES : at % LANES + p.rows]
                out[c, m, :, low:high] = piece[:, : high - low]


def lane_row(p):
    lane = lax.broadcasted_iota(jnp.int32, (SUB, p.lanes), 1)
    return lane % p.run, lane


def wrap(p, buf):
    buf[0] = roll(buf[p.step], 1, 0)
    buf[p.step + 1] = roll(buf[1], -1, 0)


def tile(t):
    return slice(t * LANES, (t + 1) * LANES)


def sheet_to(p, sheet, buf):
    def one(i, none):
        for t in range(p.tiles):
            buf[i + 1, :, tile(t)] = sheet[t, pl.ds(i, SUB, stride=p.step), :]
        return none
    lax.fori_loop(0, p.step, one, 0, unroll=p.unroll)


def to_sheet(p, buf, sheet):
    def one(i, none):
        for t in range(p.tiles):
            sheet[t, pl.ds(i, SUB, stride=p.step), :] = buf[i + 1, :, tile(t)]
        return none
    lax.fori_loop(0, p.step, one, 0, unroll=p.unroll)


def one_pass(p, src, dst, east, north, south, diag):
    def body(c, carry):
        f, fw, west = carry
        for k in range(p.stride):
            i = 1 + c * p.stride + k
            fe, here = src[i + 1], east[i]
            across = north[i] * roll(f, -1, 1) + south[i] * roll(f, 1, 1)
            dst[i] = (diag[i] * f + across) + (here * fe + west * fw)
            f, fw, west = fe, f, here
        return f, fw, west
    lax.fori_loop(0, p.step // p.stride, body, (src[1], src[0], east[0]))
    wrap(p, dst)


def ten(p, a, b, *coefs):
    def two(_, none):
        one_pass(p, a, b, *coefs)
        one_pass(p, b, a, *coefs)
        return none
    lax.fori_loop(0, PASSES // 2, two, 0)
    if PASSES % 2:
        one_pass(p, a, b, *coefs)
        a[...] = b[...]


def total_of(p, own, term):
    def one(i, acc):
        return acc + term(i + 1)
    acc = lax.fori_loop(0, p.step, one, jnp.zeros((SUB, p.lanes), jnp.float32), unroll=p.unroll)
    return jnp.sum(jnp.where(own, acc, 0.0))


def own_lanes(p):
    row, lane = lane_row(p)
    first = p.halo * p.rows
    return (row >= first) & (row < first + p.group * p.rows) & (lane < p.used)


def first_kernel(p, got, near, far, out, right, east, north, south, diag, sheet, a, b, coef):
    row, lane = lane_row(p)
    low = 0
    high = p.run - 1
    if p.groups > 1:
        here = lax.axis_index("lat") // p.group * p.group - p.halo
        low = jnp.maximum(-here, 0) * p.rows
        high = jnp.minimum(p.lat - here, p.window) * p.rows - 1
    mine = lax.axis_index("mem") % p.parts
    for k in range(max(p.parts // 2, 1)):
        coef[mine ^ k] = near[k]
    for k in range(p.parts // 2):
        coef[mine ^ (p.parts // 2) ^ k] = far[k]
    per = p.piece // LANES

    def pick(which):
        def of(c, m, cols):
            j = cols.start // LANES
            return coef[j // per, c, which, :, tile(j % per)]
        return of
    flip(p, pick(1), sheet)
    sheet_to(p, sheet, south)
    flip(p, pick(0), sheet)
    sheet_to(p, sheet, east)
    wrap(p, east)
    inside = (row >= low) & (row <= high) & (lane < p.used)

    def coefs(i, none):
        lower = jnp.where(inside, south[i + 1], 0.0)
        upper = jnp.where(inside & (row < high), roll(lower, -1, 1), 0.0)
        west = east[i]
        diag[i + 1] = (1.0 - (lower + upper)) - (east[i + 1] + west)
        north[i + 1] = upper
        south[i + 1] = jnp.where(row > low, lower, 0.0)
        return none
    lax.fori_loop(0, p.step, coefs, 0, unroll=p.unroll)
    flip(p, lambda c, m, cols: got[c, m, :, cols], sheet)
    sheet_to(p, sheet, a)
    wrap(p, a)
    ten(p, a, b, east, north, south, diag)

    def keep(i, none):
        right[i + 1] = a[i + 1]
        return none
    lax.fori_loop(0, p.step, keep, 0, unroll=p.unroll)
    rr = total_of(p, own_lanes(p), lambda i: a[i] * a[i])
    ten(p, a, b, east, north, south, diag)
    to_sheet(p, a, sheet)
    sheet[:, p.nlon :, :] = jnp.full((p.tiles, p.wide - p.nlon, LANES), rr)
    unflip(p, sheet, out, p.wide)


def second_kernel(p, got, right, east, north, south, diag, scal, out, resid, ahead, sheet, a, b):
    row, lane = lane_row(p)
    flip(p, lambda c, m, cols: got[c, m, :, cols], sheet)
    if p.groups == 1:
        q = 0.0
        for t in range(p.tiles):
            first = (row[:1, tile(t)] % p.rows == 0) & (lane[:1, tile(t)] < p.run)
            q = q + jnp.sum(jnp.where(first, sheet[t, p.nlon : p.nlon + 1, :], 0.0))
        q = jnp.full((SUB, LANES), q)
    else:
        q = scal[1][:SUB]
    rr = scal[0][:SUB]
    alpha = rr / (rr + q)
    ahead[...] = alpha
    sheet_to(p, sheet, a)
    wrap(p, a)
    ten(p, a, b, east, north, south, diag)
    alpha = jnp.broadcast_to(alpha[:, :1], (SUB, p.lanes))

    def cut(i, sums):
        r0 = right[i + 1]
        r = r0 - alpha * (r0 + a[i + 1])
        a[i + 1] = r
        resid[i + 1] = r
        return sums[0] + r * r, sums[1] + r * r0
    zero = jnp.zeros((SUB, p.lanes), jnp.float32)
    rr1, rb = lax.fori_loop(0, p.step, cut, (zero, zero), unroll=p.unroll)
    wrap(p, a)
    own = own_lanes(p)
    rr1 = jnp.sum(jnp.where(own, rr1, 0.0))
    rb = jnp.sum(jnp.where(own, rb, 0.0))
    ten(p, a, b, east, north, south, diag)
    to_sheet(p, a, sheet)
    sheet[:, p.nlon :, :] = jnp.zeros((p.tiles, p.wide - p.nlon, LANES), jnp.float32)
    sheet[:, p.nlon : p.nlon + SUB, :] = jnp.full((p.tiles, SUB, LANES), rr1)
    sheet[:, p.nlon + SUB : p.nlon + 2 * SUB, :] = jnp.full((p.tiles, SUB, LANES), rb)
    unflip(p, sheet, out, p.wide)


def back_kernel(p, field, out, sheet):
    to_sheet(p, field, sheet)
    sheet[:, p.nlon :, :] = jnp.zeros((p.tiles, p.wide - p.nlon, LANES), jnp.float32)
    unflip(p, sheet, out, p.nlon)


def buffers(p):
    buf = (p.step + 2, SUB, p.lanes)
    return [pltpu.VMEM((p.tiles, p.wide, LANES), jnp.float32)] + [pltpu.VMEM(buf, jnp.float32)] * 2


def vmem(n):
    return [pl.BlockSpec(memory_space=pltpu.VMEM)] * n


def first_half(p, got, near, far):
    buf = jax.ShapeDtypeStruct((p.step + 2, SUB, p.lanes), jnp.float32)
    back = jax.ShapeDtypeStruct((p.group, p.share, p.rows, p.wide), jnp.float32)
    coef = pltpu.VMEM((p.parts, p.window, 2, p.rows, p.piece), jnp.float32)
    return pl.pallas_call(
        functools.partial(first_kernel, p),
        in_specs=vmem(3),
        out_specs=vmem(6),
        out_shape=[back] + [buf] * 5,
        scratch_shapes=buffers(p) + [coef],
        compiler_params=ROOM,
        name="smooth_first",
    )(got, near, far)


def second_half(p, got, right, east, north, south, diag, scal):
    buf = jax.ShapeDtypeStruct((p.step + 2, SUB, p.lanes), jnp.float32)
    back = jax.ShapeDtypeStruct((p.group, p.share, p.rows, p.wide), jnp.float32)
    return pl.pallas_call(
        functools.partial(second_kernel, p),
        in_specs=vmem(7),
        out_specs=vmem(3),
        out_shape=[back, buf, jax.ShapeDtypeStruct((SUB, LANES), jnp.float32)],
        scratch_shapes=buffers(p),
        compiler_params=ROOM,
        name="smooth_second",
    )(got, right, east, north, south, diag, scal)


def to_rows(p, field):
    return pl.pallas_call(
        functools.partial(back_kernel, p),
        in_specs=vmem(1),
        out_specs=vmem(1)[0],
        out_shape=jax.ShapeDtypeStruct((p.group, p.share, p.rows, p.nlon), jnp.float32),
        scratch_shapes=buffers(p)[:1],
        cost_estimate=pl.CostEstimate(flops=0, bytes_accessed=2**22, transcendentals=0),
        compiler_params=ROOM,
        name="to_rows",
    )(field)


def scalars(p, mine, scal):
    rr1 = mine[0, :1, p.nlon : p.nlon + 1]
    rb = mine[0, :1, p.nlon + SUB : p.nlon + SUB + 1]
    rr = scal[0][:1, :1]
    beta = rr1 / rr
    return rr1, beta, rr1 + beta * (2.0 * rb + beta * rr)


def test_kernel(p, weight, total, mine, scal, part):
    at = lax.axis_index("mem") % 2 * p.half
    beta = scalars(p, mine, scal)[1]
    acc = jnp.zeros((p.rows, p.nlon), jnp.float32)
    for k in range(p.half):
        t = mine[k, :, : p.nlon] + beta * total[at + k]
        acc = acc + weight[jnp.minimum(at + k, p.fields - 1)] * t * t
    acc = jnp.broadcast_to(jnp.sum(acc, axis=(0, 1), keepdims=True), part.shape[1:])
    for k in range(part.shape[0]):
        part[k] = acc


def test(p, weight, total, mine, scal):
    copies = 1 if p.groups > 1 else p.mem * p.lat
    return pl.pallas_call(
        functools.partial(test_kernel, p),
        in_specs=vmem(4),
        out_specs=vmem(1)[0],
        out_shape=jax.ShapeDtypeStruct((copies, SUB, LANES), jnp.float32),
        compiler_params=ROOM,
        name="last_sums",
    )(weight, total, mine, scal)


def last_kernel(p, total, mine, other, scal, ahead, q, right, resid, grown, control):
    core = lax.axis_index("mem") % 2
    rr1, beta, length = scalars(p, mine, scal)
    every = q[0]
    for k in range(1, q.shape[0]):
        every = every + q[k]
    every = every[:1, :1] * (2.0 / p.mem)
    step1 = ahead[:1, :1]
    step2 = rr1 / (length + every)
    near = step1 + step2 * beta
    for half, at in ((mine, core * p.half), (other, (1 - core) * p.half)):
        for k in range(p.half):
            @pl.when(at + k < p.fields)
            def _():
                grown[at + k] = near * total[at + k] + step2 * half[k, :, : p.nlon]
    for m in range(p.members):
        control[m] = near * right[m] + step2 * resid[m]


def last(p, total, mine, other, scal, ahead, q, right, resid):
    return pl.pallas_call(
        functools.partial(last_kernel, p),
        in_specs=vmem(8),
        out_specs=vmem(2),
        out_shape=[
            jax.ShapeDtypeStruct((p.fields, p.rows, p.nlon), jnp.float32),
            jax.ShapeDtypeStruct((p.members, p.rows, p.nlon), jnp.float32),
        ],
        compiler_params=ROOM,
        name="last_update",
    )(total, mine, other, scal, ahead, q, right, resid)


def swap(p, x, axis, bit, count):
    return lax.ppermute(x, axis, [(i, i ^ bit) for i in range(count)])


def turn(p, x):
    if p.groups == 1:
        return lax.all_to_all(x, "lat", 0, 0)
    sets = [[g * p.group + i for i in range(p.group)] for g in range(p.groups)]
    return lax.all_to_all(x, "lat", 0, 0, axis_index_groups=sets)


def widen(p, x):
    if p.groups == 1:
        return x
    gap = p.group
    up = [(i, i + gap) for i in range(p.lat - gap)]
    down = [(i + gap, i) for i in range(p.lat - gap)]
    before = lax.ppermute(x[-p.halo :], "lat", up)
    after = lax.ppermute(x[: p.halo], "lat", down)
    return jnp.concatenate([before, x, after], axis=0)


def member_sum(p, keep, send):
    mine = keep + swap(p, send, "mem", 1, p.mem)
    bit = 2
    while bit < p.mem:
        mine = mine + swap(p, mine, "mem", bit, p.mem)
        bit *= 2
    if p.groups > 1:
        tail = lax.psum(mine[:1, :, p.nlon :], "lat") / p.group
        mine = lax.dynamic_update_slice(mine, tail, (0, 0, p.nlon))
    return mine


def coefficients(p, lon_coef, lat_coef):
    both = jnp.pad(jnp.stack([lon_coef, lat_coef]), ((0, 0), (0, 0), (0, p.wide - p.nlon)))
    part = lax.axis_index("mem") % p.parts
    both = lax.dynamic_slice_in_dim(both, part * p.piece, p.piece, axis=2)
    both = jnp.broadcast_to(both[None], (p.group, 2, p.rows, p.piece))
    near = widen(p, turn(p, both))[None]
    if p.parts == 1:
        return near, near
    if p.parts == 4:
        near = jnp.concatenate([near, swap(p, near, "mem", 1, p.mem)])
    return near, swap(p, near, "mem", p.parts // 2, p.mem)


def per_device(perturb, innovation, obs_weight, lon_coef, lat_coef):
    p = Plan(perturb, lat_coef, lax.axis_size("mem"), lax.axis_size("lat"))
    flat = lambda x: x.reshape(p.fields, p.rows, p.nlon)
    by_rank = lambda x: x.reshape((p.members,) + x.shape[2:])
    weight = flat(obs_weight)
    by_member = perturb.reshape(p.members, p.fields, p.rows, p.nlon)

    near, far = coefficients(p, lon_coef, lat_coef)
    (sent,) = adjoint(p, by_member, weight, flat(innovation), second=False)
    back, right, *coefs = first_half(p, widen(p, turn(p, sent)), near, far)
    field, rows_right = lax.optimization_barrier((turn(p, back), to_rows(p, right)))
    rows_right = by_rank(turn(p, rows_right))
    mine = member_sum(p, *forward(p, perturb, by_rank(field)))
    other = swap(p, mine, "mem", 1, p.mem)
    sent, total, scal = adjoint(p, by_member, weight, mine, other, second=True)
    sent, rows_right = lax.optimization_barrier((sent, rows_right))
    if p.groups > 1:
        scal = jnp.concatenate([scal[:1], lax.psum(scal[1:], "lat")], axis=0)
    back, resid, ahead = second_half(p, widen(p, turn(p, sent)), right, *coefs, scal)
    field, rows_resid = lax.optimization_barrier((turn(p, back), to_rows(p, resid)))
    rows_resid = by_rank(turn(p, rows_resid))
    mine = member_sum(p, *forward(p, perturb, by_rank(field)))
    mine, rows_resid = lax.optimization_barrier((mine, rows_resid))
    other = swap(p, mine, "mem", 1, p.mem)
    q = test(p, weight, total, mine, scal)
    q = lax.all_to_all(q, ("mem", "lat"), 0, 0) if p.groups == 1 else lax.psum(q, ("mem", "lat"))
    grown, control = last(p, total, mine, other, scal, ahead, q, rows_right, rows_resid)
    return control, grown.reshape(p.slots, p.vars, p.rows, p.nlon)


def solution(mesh):
    return jax.shard_map(
        per_device,
        mesh=mesh,
        in_specs=(
            P("mem", None, None, "lat", None),
            P(None, None, "lat", None),
            P(None, None, "lat", None),
            P("lat", None),
            P("lat", None),
        ),
        out_specs=(P("mem", "lat", None), P(None, None, "lat", None)),
        check_vma=False,
    )
```

```python
import functools

import jax
import jax.numpy as jnp
from jax import lax
from jax.experimental import pallas as pl
from jax.experimental.pallas import tpu as pltpu
from jax.sharding import PartitionSpec as P

PASSES = 10
LANES = 128
SUB = 8
ROOM = pltpu.CompilerParams(vmem_limit_bytes=24 * 2**20)


def ceil_to(value, unit):
    return -(-value // unit) * unit


class Plan:
    def __init__(self, perturb, lat_coef, mem, lat):
        self.members, self.slots, self.vars, self.rows, self.nlon = perturb.shape
        self.mem, self.lat = mem, lat
        self.fields = self.slots * self.vars
        self.half = (self.fields + 2) // 2
        self.wide = ceil_to(self.nlon + 16, LANES)
        halo = -(-2 * PASSES // self.rows)
        self.group = max(
            g for g in range(1, lat + 1)
            if lat % g == 0 and self.members % g == 0 and (g == lat or g >= halo)
        )
        self.groups = lat // self.group
        self.halo = 0 if self.groups == 1 else halo
        self.share = self.members // self.group
        self.window = self.group + 2 * self.halo
        self.run = self.window * self.rows
        self.used = self.share * self.run
        self.lanes = ceil_to(self.used, LANES)
        self.tiles = self.lanes // LANES
        self.step = self.nlon // SUB
        self.unroll = max(u for u in range(1, 21) if self.step % u == 0)
        self.stride = max(u for u in range(1, 181) if self.step % u == 0)
        self.parts = max(
            q for q in (1, 2, 4) if mem % q == 0 and self.wide % (q * LANES) == 0
        )
        self.piece = self.wide // self.parts


def adjoint_kernel(p, second, *refs):
    if second:
        perturb, weight, mine, other, out, total, scal, prod = refs
    else:
        perturb, weight, value, out, prod = refs
    step = pl.program_id(0)

    @pl.when(step == 0)
    def _():
        if second:
            core = lax.axis_index("mem") % 2
            acc = jnp.zeros((p.rows, p.nlon), jnp.float32)
            for half, at in ((mine, core * p.half), (other, (1 - core) * p.half)):
                for k in range(p.half):
                    t = half[k, :, : p.nlon]
                    wt = weight[jnp.minimum(at + k, p.fields - 1)] * t
                    prod[at + k] = wt
                    total[at + k] = t
                    acc = acc + wt * t
            rr = mine[0, :1, p.nlon : p.nlon + 1]
            scal[0] = jnp.broadcast_to(rr, (p.rows, LANES))
            scal[1] = jnp.full((p.rows, LANES), jnp.sum(acc))
        else:
            for k in range(p.fields):
                prod[k] = weight[k] * value[k]

    acc = [0.0] * p.share
    for k in range(p.fields):
        row = prod[k]
        for m in range(p.share):
            acc[m] = acc[m] + perturb[m, k].astype(jnp.float32) * row
    tail = jnp.zeros((p.rows, p.wide - p.nlon), jnp.float32)
    if second:
        tail = jnp.broadcast_to(scal[1][:1, :1], tail.shape)
    for m in range(p.share):
        out[0, m, :, : p.nlon] = acc[m]
        out[0, m, :, p.nlon :] = tail


def adjoint(p, perturb, weight, *rest, second):
    whole = lambda *shape: pl.BlockSpec(shape, lambda i: (0,) * len(shape))
    rows, nlon = p.rows, p.nlon
    field = whole(p.fields, rows, nlon)
    more = [whole(p.half, rows, p.wide)] * 2 if second else [field]
    out_shape = [jax.ShapeDtypeStruct((p.group, p.share, rows, p.wide), jnp.float32)]
    out_specs = [pl.BlockSpec((1, p.share, rows, p.wide), lambda i: (i, 0, 0, 0))]
    if second:
        out_shape += [
            jax.ShapeDtypeStruct((2 * p.half, rows, nlon), jnp.float32),
            jax.ShapeDtypeStruct((2, rows, LANES), jnp.float32),
        ]
        out_specs += [whole(2 * p.half, rows, nlon), whole(2, rows, LANES)]
    return pl.pallas_call(
        functools.partial(adjoint_kernel, p, second),
        grid=(p.group,),
        in_specs=[
            pl.BlockSpec((p.share, p.fields, rows, nlon), lambda i: (i, 0, 0, 0)),
            field,
            *more,
        ],
        out_specs=out_specs,
        out_shape=out_shape,
        scratch_shapes=[pltpu.VMEM((2 * p.half, rows, nlon), jnp.float32)],
        cost_estimate=cost(p, 2),
        compiler_params=ROOM,
        name="adjoint_second" if second else "adjoint_first",
    )(perturb, weight, *rest)


def cost(p, size):
    cells = p.members * p.fields * p.rows * p.nlon
    return pl.CostEstimate(flops=2 * cells, bytes_accessed=size * cells, transcendentals=0)


def forward_kernel(p, perturb, field, keep, send, scr):
    step = pl.program_id(0)

    @pl.when(step == 0)
    def _():
        for k in range(2 * p.half):
            scr[k, :, p.nlon :] = jnp.zeros((p.rows, p.wide - p.nlon), jnp.float32)
        for k in range(p.fields, 2 * p.half):
            scr[k, :, : p.nlon] = jnp.zeros((p.rows, p.nlon), jnp.float32)

    split = p.nlon // (2 * LANES) * LANES
    for cols in (slice(0, split), slice(split, p.nlon)):
        acc = [0.0] * p.vars
        for m in range(p.members):
            f = field[m, :, cols]
            for v in range(p.vars):
                acc[v] = acc[v] + perturb[m, 0, v, :, cols].astype(jnp.float32) * f
        for v in range(p.vars):
            scr[step * p.vars + v, :, cols] = acc[v]

    @pl.when(step == p.slots - 1)
    def _():
        core = lax.axis_index("mem") % 2
        one = jnp.zeros((1, 1), jnp.float32)
        two = jnp.zeros((1, 1), jnp.float32)
        for k in range(p.group):
            one = one + field[k * p.share, :1, p.nlon : p.nlon + 1]
            two = two + field[k * p.share, :1, p.nlon + SUB : p.nlon + SUB + 1]
        for k in (0, p.half):
            scr[k, :, p.nlon : p.nlon + SUB] = jnp.broadcast_to(one, (p.rows, SUB))
            scr[k, :, p.nlon + SUB : p.nlon + 2 * SUB] = jnp.broadcast_to(two, (p.rows, SUB))
        for k in range(p.half):
            keep[k] = scr[core * p.half + k]
            send[k] = scr[(1 - core) * p.half + k]


def forward(p, perturb, field):
    rows, nlon = p.rows, p.nlon
    shape = (p.half, rows, p.wide)
    spec = pl.BlockSpec(shape, lambda i: (0, 0, 0))
    return pl.pallas_call(
        functools.partial(forward_kernel, p),
        grid=(p.slots,),
        in_specs=[
            pl.BlockSpec((p.members, 1, p.vars, rows, nlon), lambda i: (0, i, 0, 0, 0)),
            pl.BlockSpec((p.members, rows, p.wide), lambda i: (0, 0, 0)),
        ],
        out_specs=[spec, spec],
        out_shape=[jax.ShapeDtypeStruct(shape, jnp.float32)] * 2,
        scratch_shapes=[pltpu.VMEM((2 * p.half, rows, p.wide), jnp.float32)],
        cost_estimate=cost(p, 2),
        compiler_params=ROOM,
        name="forward",
    )(perturb, field)


def roll(x, shift, axis):
    return pltpu.roll(x, shift % x.shape[axis], axis)


def flip(p, pick, sheet):
    for j in range(p.wide // LANES):
        cols = slice(j * LANES, (j + 1) * LANES)
        tiles = [pick(c, m, cols) for m in range(p.share) for c in range(p.window)]
        if p.used < p.lanes:
            tiles.append(jnp.zeros((p.lanes - p.used, LANES), jnp.float32))
        block = jnp.concatenate(tiles, axis=0)
        for t in range(p.tiles):
            sheet[t, cols, :] = block[t * LANES : (t + 1) * LANES].T


def unflip(p, sheet, out, stop):
    for j in range(-(-stop // LANES)):
        low, high = j * LANES, min((j + 1) * LANES, stop)
        block = [sheet[t, low : low + LANES, :].T for t in range(p.tiles)]
        for m in range(p.share):
            for c in range(p.group):
                at = m * p.run + (p.halo + c) * p.rows
                piece = block[at // LANES][at % LANES : at % LANES + p.rows]
                out[c, m, :, low:high] = piece[:, : high - low]


def lane_row(p):
    lane = lax.broadcasted_iota(jnp.int32, (SUB, p.lanes), 1)
    return lane % p.run, lane


def wrap(p, buf):
    buf[0] = roll(buf[p.step], 1, 0)
    buf[p.step + 1] = roll(buf[1], -1, 0)


def tile(t):
    return slice(t * LANES, (t + 1) * LANES)


def sheet_to(p, sheet, buf):
    def one(i, none):
        for t in range(p.tiles):
            buf[i + 1, :, tile(t)] = sheet[t, pl.ds(i, SUB, stride=p.step), :]
        return none
    lax.fori_loop(0, p.step, one, 0, unroll=p.unroll)


def to_sheet(p, buf, sheet):
    def one(i, none):
        for t in range(p.tiles):
            sheet[t, pl.ds(i, SUB, stride=p.step), :] = buf[i + 1, :, tile(t)]
        return none
    lax.fori_loop(0, p.step, one, 0, unroll=p.unroll)


def one_pass(p, src, dst, east, north, south, diag):
    def body(c, carry):
        f, fw, west = carry
        for k in range(p.stride):
            i = 1 + c * p.stride + k
            fe, here = src[i + 1], east[i]
            across = north[i] * roll(f, -1, 1) + south[i] * roll(f, 1, 1)
            dst[i] = (diag[i] * f + across) + (here * fe + west * fw)
            f, fw, west = fe, f, here
        return f, fw, west
    lax.fori_loop(0, p.step // p.stride, body, (src[1], src[0], east[0]))
    wrap(p, dst)


def ten(p, a, b, *coefs):
    def two(_, none):
        one_pass(p, a, b, *coefs)
        one_pass(p, b, a, *coefs)
        return none
    lax.fori_loop(0, PASSES // 2, two, 0)
    if PASSES % 2:
        one_pass(p, a, b, *coefs)
        a[...] = b[...]


def total_of(p, own, term):
    def one(i, acc):
        return acc + term(i + 1)
    acc = lax.fori_loop(0, p.step, one, jnp.zeros((SUB, p.lanes), jnp.float32), unroll=p.unroll)
    return jnp.sum(jnp.where(own, acc, 0.0))


def own_lanes(p):
    row, lane = lane_row(p)
    first = p.halo * p.rows
    return (row >= first) & (row < first + p.group * p.rows) & (lane < p.used)


def ends(p):
    if p.groups == 1:
        return 0, p.run - 1
    here = lax.axis_index("lat") // p.group * p.group - p.halo
    return jnp.maximum(-here, 0) * p.rows, jnp.minimum(p.lat - here, p.window) * p.rows - 1


def spread(p, low, high, lower, east, north, south, diag):
    row, lane = lane_row(p)

    def coefs(i, none):
        below = lower[i + 1]
        above = jnp.where(row < high, roll(below, -1, 1), 0.0)
        diag[i + 1] = (1.0 - (below + above)) - (east[i + 1] + east[i])
        north[i + 1] = above
        south[i + 1] = jnp.where(row > low, below, 0.0)
        return none
    lax.fori_loop(0, p.step, coefs, 0, unroll=p.unroll)


def first_kernel(p, got, near, far, out, *refs):
    stores, sheet, a, b, north, south, diag, right, east, lower, rows_right, coef, sem = (
        refs[:4], *refs[4:]
    )
    row, lane = lane_row(p)
    low, high = ends(p)
    mine = lax.axis_index("mem") % p.parts
    for k in range(max(p.parts // 2, 1)):
        coef[mine ^ k] = near[k]
    for k in range(p.parts // 2):
        coef[mine ^ (p.parts // 2) ^ k] = far[k]
    per = p.piece // LANES

    def pick(which):
        def of(c, m, cols):
            j = cols.start // LANES
            return coef[j // per, c, which, :, tile(j % per)]
        return of
    flip(p, pick(1), sheet)
    sheet_to(p, sheet, lower)
    flip(p, pick(0), sheet)
    sheet_to(p, sheet, east)
    wrap(p, east)
    inside = (row >= low) & (row <= high) & (lane < p.used)

    def clean(i, none):
        lower[i + 1] = jnp.where(inside, lower[i + 1], 0.0)
        return none
    lax.fori_loop(0, p.step, clean, 0, unroll=p.unroll)
    spread(p, low, high, lower, east, north, south, diag)
    flip(p, lambda c, m, cols: got[c, m, :, cols], sheet)
    sheet_to(p, sheet, a)
    wrap(p, a)
    ten(p, a, b, east, north, south, diag)

    def keep(i, none):
        right[i + 1] = a[i + 1]
        return none
    lax.fori_loop(0, p.step, keep, 0, unroll=p.unroll)
    rr = total_of(p, own_lanes(p), lambda i: a[i] * a[i])
    to_sheet(p, a, sheet)
    unflip(p, sheet, rows_right, p.nlon)
    moves = [
        pltpu.make_async_copy(src, dst, sem.at[k])
        for k, (src, dst) in enumerate(zip((rows_right, right, east, lower), stores))
    ]
    for move in moves:
        move.start()
    ten(p, a, b, east, north, south, diag)
    to_sheet(p, a, sheet)
    sheet[:, p.nlon :, :] = jnp.full((p.tiles, p.wide - p.nlon, LANES), rr)
    unflip(p, sheet, out, p.wide)
    for move in moves:
        move.wait()


def second_kernel(p, got, scal, *refs):
    loads, out, store, ahead, sheet, a, b, north, south, diag, right, east, lower, rows_resid, sem = (
        refs[:3], *refs[3:]
    )
    row, lane = lane_row(p)
    moves = [
        pltpu.make_async_copy(src, dst, sem.at[k])
        for k, (src, dst) in enumerate(zip(loads, (east, lower, right)))
    ]
    for move in moves:
        move.start()
    flip(p, lambda c, m, cols: got[c, m, :, cols], sheet)
    if p.groups == 1:
        q = 0.0
        for t in range(p.tiles):
            first = (row[:1, tile(t)] % p.rows == 0) & (lane[:1, tile(t)] < p.run)
            q = q + jnp.sum(jnp.where(first, sheet[t, p.nlon : p.nlon + 1, :], 0.0))
        q = jnp.full((SUB, LANES), q)
    else:
        q = scal[1][:SUB]
    rr = scal[0][:SUB]
    alpha = rr / (rr + q)
    ahead[...] = alpha
    sheet_to(p, sheet, a)
    wrap(p, a)
    moves[0].wait()
    moves[1].wait()
    spread(p, *ends(p), lower, east, north, south, diag)
    ten(p, a, b, east, north, south, diag)
    moves[2].wait()
    alpha = jnp.broadcast_to(alpha[:, :1], (SUB, p.lanes))

    def cut(i, sums):
        r0 = right[i + 1]
        r = r0 - alpha * (r0 + a[i + 1])
        a[i + 1] = r
        return sums[0] + r * r, sums[1] + r * r0
    zero = jnp.zeros((SUB, p.lanes), jnp.float32)
    rr1, rb = lax.fori_loop(0, p.step, cut, (zero, zero), unroll=p.unroll)
    wrap(p, a)
    own = own_lanes(p)
    rr1 = jnp.sum(jnp.where(own, rr1, 0.0))
    rb = jnp.sum(jnp.where(own, rb, 0.0))
    to_sheet(p, a, sheet)
    unflip(p, sheet, rows_resid, p.nlon)
    leave = pltpu.make_async_copy(rows_resid, store, sem.at[3])
    leave.start()
    ten(p, a, b, east, north, south, diag)
    to_sheet(p, a, sheet)
    sheet[:, p.nlon :, :] = jnp.zeros((p.tiles, p.wide - p.nlon, LANES), jnp.float32)
    sheet[:, p.nlon : p.nlon + SUB, :] = jnp.full((p.tiles, SUB, LANES), rr1)
    sheet[:, p.nlon + SUB : p.nlon + 2 * SUB, :] = jnp.full((p.tiles, SUB, LANES), rb)
    unflip(p, sheet, out, p.wide)
    leave.wait()


def vmem(n):
    return [pl.BlockSpec(memory_space=pltpu.VMEM)] * n


def hbm(n):
    return [pl.BlockSpec(memory_space=pltpu.HBM)] * n


def half_shapes(p):
    buf = (p.step + 2, SUB, p.lanes)
    rows = (p.group, p.share, p.rows, p.nlon)
    back = (p.group, p.share, p.rows, p.wide)
    scratch = [pltpu.VMEM((p.tiles, p.wide, LANES), jnp.float32)]
    scratch += [pltpu.VMEM(buf, jnp.float32)] * 8
    scratch += [pltpu.VMEM(rows, jnp.float32)]
    return *(jax.ShapeDtypeStruct(x, jnp.float32) for x in (buf, rows, back)), scratch


def first_half(p, got, near, far):
    buf, rows, back, scratch = half_shapes(p)
    coef = pltpu.VMEM((p.parts, p.window, 2, p.rows, p.piece), jnp.float32)
    return pl.pallas_call(
        functools.partial(first_kernel, p),
        in_specs=vmem(3),
        out_specs=vmem(1) + hbm(4),
        out_shape=[back] + [pltpu.HBM(x.shape, x.dtype) for x in (rows, buf, buf, buf)],
        scratch_shapes=scratch + [coef, pltpu.SemaphoreType.DMA((4,))],
        compiler_params=ROOM,
        name="smooth_first",
    )(got, near, far)


def second_half(p, got, scal, right, east, lower):
    buf, rows, back, scratch = half_shapes(p)
    return pl.pallas_call(
        functools.partial(second_kernel, p),
        in_specs=vmem(2) + hbm(3),
        out_specs=vmem(1) + hbm(1) + vmem(1),
        out_shape=[
            back,
            pltpu.HBM(rows.shape, rows.dtype),
            jax.ShapeDtypeStruct((SUB, LANES), jnp.float32),
        ],
        scratch_shapes=scratch + [pltpu.SemaphoreType.DMA((4,))],
        compiler_params=ROOM,
        name="smooth_second",
    )(got, scal, *(pltpu.with_memory_space_constraint(x, pltpu.HBM) for x in (east, lower, right)))


def scalars(p, mine, scal):
    rr1 = mine[0, :1, p.nlon : p.nlon + 1]
    rb = mine[0, :1, p.nlon + SUB : p.nlon + SUB + 1]
    rr = scal[0][:1, :1]
    beta = rr1 / rr
    return rr1, beta, rr1 + beta * (2.0 * rb + beta * rr)


def test_kernel(p, weight, total, mine, scal, part):
    at = lax.axis_index("mem") % 2 * p.half
    beta = scalars(p, mine, scal)[1]
    acc = jnp.zeros((p.rows, p.nlon), jnp.float32)
    for k in range(p.half):
        t = mine[k, :, : p.nlon] + beta * total[at + k]
        acc = acc + weight[jnp.minimum(at + k, p.fields - 1)] * t * t
    acc = jnp.broadcast_to(jnp.sum(acc, axis=(0, 1), keepdims=True), part.shape[1:])
    for k in range(part.shape[0]):
        part[k] = acc


def test(p, weight, total, mine, scal):
    copies = 1 if p.groups > 1 else p.mem * p.lat
    return pl.pallas_call(
        functools.partial(test_kernel, p),
        in_specs=vmem(4),
        out_specs=vmem(1)[0],
        out_shape=jax.ShapeDtypeStruct((copies, SUB, LANES), jnp.float32),
        compiler_params=ROOM,
        name="last_sums",
    )(weight, total, mine, scal)


def last_kernel(p, total, mine, other, scal, ahead, q, right, resid, grown, control):
    core = lax.axis_index("mem") % 2
    rr1, beta, length = scalars(p, mine, scal)
    every = q[0]
    for k in range(1, q.shape[0]):
        every = every + q[k]
    every = every[:1, :1] * (2.0 / p.mem)
    step1 = ahead[:1, :1]
    step2 = rr1 / (length + every)
    near = step1 + step2 * beta
    for half, at in ((mine, core * p.half), (other, (1 - core) * p.half)):
        for k in range(p.half):
            @pl.when(at + k < p.fields)
            def _():
                grown[at + k] = near * total[at + k] + step2 * half[k, :, : p.nlon]
    for m in range(p.members):
        control[m] = near * right[m] + step2 * resid[m]


def last(p, total, mine, other, scal, ahead, q, right, resid):
    return pl.pallas_call(
        functools.partial(last_kernel, p),
        in_specs=vmem(8),
        out_specs=vmem(2),
        out_shape=[
            jax.ShapeDtypeStruct((p.fields, p.rows, p.nlon), jnp.float32),
            jax.ShapeDtypeStruct((p.members, p.rows, p.nlon), jnp.float32),
        ],
        compiler_params=ROOM,
        name="last_update",
    )(total, mine, other, scal, ahead, q, right, resid)


def swap(p, x, axis, bit, count):
    return lax.ppermute(x, axis, [(i, i ^ bit) for i in range(count)])


def turn(p, x):
    if p.groups == 1:
        return lax.all_to_all(x, "lat", 0, 0)
    sets = [[g * p.group + i for i in range(p.group)] for g in range(p.groups)]
    return lax.all_to_all(x, "lat", 0, 0, axis_index_groups=sets)


def widen(p, x):
    if p.groups == 1:
        return x
    gap = p.group
    up = [(i, i + gap) for i in range(p.lat - gap)]
    down = [(i + gap, i) for i in range(p.lat - gap)]
    before = lax.ppermute(x[-p.halo :], "lat", up)
    after = lax.ppermute(x[: p.halo], "lat", down)
    return jnp.concatenate([before, x, after], axis=0)


def member_sum(p, keep, send):
    mine = keep + swap(p, send, "mem", 1, p.mem)
    bit = 2
    while bit < p.mem:
        mine = mine + swap(p, mine, "mem", bit, p.mem)
        bit *= 2
    if p.groups > 1:
        tail = lax.psum(mine[:1, :, p.nlon :], "lat") / p.group
        mine = lax.dynamic_update_slice(mine, tail, (0, 0, p.nlon))
    return mine


def coefficients(p, lon_coef, lat_coef):
    both = jnp.pad(jnp.stack([lon_coef, lat_coef]), ((0, 0), (0, 0), (0, p.wide - p.nlon)))
    part = lax.axis_index("mem") % p.parts
    both = lax.dynamic_slice_in_dim(both, part * p.piece, p.piece, axis=2)
    return turn(p, jnp.broadcast_to(both[None], (p.group, 2, p.rows, p.piece)))


def share_out(p, pieces):
    near = widen(p, pieces)[None]
    if p.parts == 1:
        return near, near
    if p.parts == 4:
        near = jnp.concatenate([near, swap(p, near, "mem", 1, p.mem)])
    return near, swap(p, near, "mem", p.parts // 2, p.mem)


def per_device(perturb, innovation, obs_weight, lon_coef, lat_coef):
    p = Plan(perturb, lat_coef, lax.axis_size("mem"), lax.axis_size("lat"))
    flat = lambda x: x.reshape(p.fields, p.rows, p.nlon)
    by_rank = lambda x: x.reshape((p.members,) + x.shape[2:])
    weight = flat(obs_weight)
    by_member = perturb.reshape(p.members, p.fields, p.rows, p.nlon)

    pieces, value = lax.optimization_barrier((coefficients(p, lon_coef, lat_coef), flat(innovation)))
    (sent,) = adjoint(p, by_member, weight, value, second=False)
    near, far = share_out(p, pieces)
    back, rows_right, *kept = first_half(p, widen(p, turn(p, sent)), near, far)
    field, rows_right = lax.optimization_barrier((turn(p, back), rows_right))
    with jax.named_scope("return_first"):
        rows_right = by_rank(turn(p, rows_right))
    with jax.named_scope("map_first"):
        keep, send = forward(p, perturb, by_rank(field))
    mine = member_sum(p, keep, send)
    other = swap(p, mine, "mem", 1, p.mem)
    sent, total, scal = adjoint(p, by_member, weight, mine, other, second=True)
    sent, rows_right = lax.optimization_barrier((sent, rows_right))
    if p.groups > 1:
        scal = jnp.concatenate([scal[:1], lax.psum(scal[1:], "lat")], axis=0)
    back, rows_resid, ahead = second_half(p, widen(p, turn(p, sent)), scal, *kept)
    field, rows_resid = lax.optimization_barrier((turn(p, back), rows_resid))
    with jax.named_scope("return_second"):
        rows_resid = by_rank(turn(p, rows_resid))
    with jax.named_scope("map_second"):
        keep, send = forward(p, perturb, by_rank(field))
    mine = member_sum(p, keep, send)
    mine, rows_resid = lax.optimization_barrier((mine, rows_resid))
    other = swap(p, mine, "mem", 1, p.mem)
    q = test(p, weight, total, mine, scal)
    q = lax.all_to_all(q, ("mem", "lat"), 0, 0) if p.groups == 1 else lax.psum(q, ("mem", "lat"))
    grown, control = last(p, total, mine, other, scal, ahead, q, rows_right, rows_resid)
    return control, grown.reshape(p.slots, p.vars, p.rows, p.nlon)


def solution(mesh):
    return jax.shard_map(
        per_device,
        mesh=mesh,
        in_specs=(
            P("mem", None, None, "lat", None),
            P(None, None, "lat", None),
            P(None, None, "lat", None),
            P("lat", None),
            P("lat", None),
        ),
        out_specs=(P("mem", "lat", None), P(None, None, "lat", None)),
        check_vma=False,
    )
```

```python
import functools

import jax
import jax.numpy as jnp
from jax import lax
from jax.experimental import pallas as pl
from jax.experimental.pallas import tpu as pltpu
from jax.sharding import PartitionSpec as P

PASSES = 10
LANES = 128
SUB = 8
ROOM = pltpu.CompilerParams(vmem_limit_bytes=24 * 2**20)


def ceil_to(value, unit):
    return -(-value // unit) * unit


class Plan:
    def __init__(self, perturb, lat_coef, mem, lat):
        self.members, self.slots, self.vars, self.rows, self.nlon = perturb.shape
        self.mem, self.lat = mem, lat
        self.fields = self.slots * self.vars
        self.half = (self.fields + 2) // 2
        self.wide = ceil_to(self.nlon + 16, LANES)
        halo = -(-2 * PASSES // self.rows)
        self.group = max(
            g for g in range(1, lat + 1)
            if lat % g == 0 and self.members % g == 0 and (g == lat or g >= halo)
        )
        self.groups = lat // self.group
        self.halo = 0 if self.groups == 1 else halo
        self.share = self.members // self.group
        self.window = self.group + 2 * self.halo
        self.run = self.window * self.rows
        self.used = self.share * self.run
        self.lanes = ceil_to(self.used, LANES)
        self.tiles = self.lanes // LANES
        self.step = self.nlon // SUB
        self.unroll = max(u for u in range(1, 21) if self.step % u == 0)
        self.stride = max(u for u in range(1, 181) if self.step % u == 0)
        self.parts = max(
            q for q in (1, 2, 4) if mem % q == 0 and self.wide % (q * LANES) == 0
        )
        self.piece = self.wide // self.parts


def mapped(p, perturb, first, prod):
    acc = [0.0] * p.share
    for k in range(p.fields):
        row = prod[k]
        for m in range(p.share):
            acc[m] = acc[m] + perturb[first + m, k].astype(jnp.float32) * row
    return acc


def adjoint_first_kernel(p, perturb, weight, value, out, pbuf, wbuf, vbuf, obuf, prod, sem):
    def part(k):
        rows = pl.ds(k * p.share, p.share)
        return pltpu.make_async_copy(perturb.at[rows], pbuf.at[rows], sem.at[k])

    def leave(k):
        return pltpu.make_async_copy(obuf.at[k], out.at[k], sem.at[p.group + k])

    heads = [
        pltpu.make_async_copy(weight, wbuf, sem.at[2 * p.group]),
        pltpu.make_async_copy(value, vbuf, sem.at[2 * p.group + 1]),
    ]
    for head in heads:
        head.start()
    for k in range(p.group):
        part(k).start()
    for head in heads:
        head.wait()
    for k in range(p.fields):
        prod[k] = wbuf[k] * vbuf[k]

    def one(k, none):
        part(k).wait()
        acc = mapped(p, pbuf, k * p.share, prod)
        for m in range(p.share):
            obuf[k, m, :, : p.nlon] = acc[m]
            obuf[k, m, :, p.nlon :] = jnp.zeros((p.rows, p.wide - p.nlon), jnp.float32)
        leave(k).start()
        return none
    lax.fori_loop(0, p.group, one, 0)
    for k in range(p.group):
        leave(k).wait()


def adjoint_first(p, perturb, weight, value):
    shape = (p.group, p.share, p.rows, p.wide)
    field = pltpu.VMEM((p.fields, p.rows, p.nlon), jnp.float32)
    held = [pltpu.with_memory_space_constraint(x, pltpu.HBM) for x in (perturb, weight, value)]
    return pl.pallas_call(
        functools.partial(adjoint_first_kernel, p),
        in_specs=hbm(3),
        out_specs=hbm(1)[0],
        out_shape=pltpu.HBM(shape, jnp.float32),
        scratch_shapes=[
            pltpu.VMEM(perturb.shape, perturb.dtype),
            field,
            field,
            pltpu.VMEM(shape, jnp.float32),
            field,
            pltpu.SemaphoreType.DMA((2 * p.group + 2,)),
        ],
        compiler_params=ROOM,
        cost_estimate=cost(p, 2),
        name="adjoint_first",
    )(*held)


def adjoint_kernel(p, perturb, weight, mine, other, out, total, scal, prod):
    step = pl.program_id(0)

    @pl.when(step == 0)
    def _():
        core = lax.axis_index("mem") % 2
        acc = jnp.zeros((p.rows, p.nlon), jnp.float32)
        for half, at in ((mine, core * p.half), (other, (1 - core) * p.half)):
            for k in range(p.half):
                t = half[k, :, : p.nlon]
                wt = weight[jnp.minimum(at + k, p.fields - 1)] * t
                prod[at + k] = wt
                total[at + k] = t
                acc = acc + wt * t
        rr = mine[0, :1, p.nlon : p.nlon + 1]
        scal[0] = jnp.broadcast_to(rr, (p.rows, LANES))
        scal[1] = jnp.full((p.rows, LANES), jnp.sum(acc))

    acc = mapped(p, perturb, 0, prod)
    tail = jnp.broadcast_to(scal[1][:1, :1], (p.rows, p.wide - p.nlon))
    for m in range(p.share):
        out[0, m, :, : p.nlon] = acc[m]
        out[0, m, :, p.nlon :] = tail


def adjoint(p, perturb, weight, mine, other):
    whole = lambda *shape: pl.BlockSpec(shape, lambda i: (0,) * len(shape))
    rows, nlon = p.rows, p.nlon
    return pl.pallas_call(
        functools.partial(adjoint_kernel, p),
        grid=(p.group,),
        in_specs=[
            pl.BlockSpec((p.share, p.fields, rows, nlon), lambda i: (i, 0, 0, 0)),
            whole(p.fields, rows, nlon),
            whole(p.half, rows, p.wide),
            whole(p.half, rows, p.wide),
        ],
        out_specs=[
            pl.BlockSpec((1, p.share, rows, p.wide), lambda i: (i, 0, 0, 0)),
            whole(2 * p.half, rows, nlon),
            whole(2, rows, LANES),
        ],
        out_shape=[
            jax.ShapeDtypeStruct((p.group, p.share, rows, p.wide), jnp.float32),
            jax.ShapeDtypeStruct((2 * p.half, rows, nlon), jnp.float32),
            jax.ShapeDtypeStruct((2, rows, LANES), jnp.float32),
        ],
        scratch_shapes=[pltpu.VMEM((2 * p.half, rows, nlon), jnp.float32)],
        compiler_params=ROOM,
        cost_estimate=cost(p, 2),
        name="adjoint_second",
    )(perturb, weight, mine, other)


def cost(p, size):
    cells = p.members * p.fields * p.rows * p.nlon
    return pl.CostEstimate(flops=2 * cells, bytes_accessed=size * cells, transcendentals=0)


def forward_kernel(p, perturb, field, keep, send, held, scr, sem):
    cut = -(-p.vars // 2)
    parts = [(t, 0, p.vars) for t in range(p.slots - 1)]
    parts += [(p.slots - 1, 0, cut), (p.slots - 1, cut, p.vars)]
    moves = []
    for n, (t, low, high) in enumerate(parts):
        at = (slice(None), t, pl.ds(low, high - low))
        moves.append(pltpu.make_async_copy(perturb.at[at], held.at[at], sem.at[n]))
        moves[-1].start()

    one = jnp.zeros((1, 1), jnp.float32)
    two = jnp.zeros((1, 1), jnp.float32)
    for k in range(p.group):
        one = one + field[k * p.share, :1, p.nlon : p.nlon + 1]
        two = two + field[k * p.share, :1, p.nlon + SUB : p.nlon + SUB + 1]
    for k in range(2 * p.half):
        scr[k, :, p.nlon :] = jnp.zeros((p.rows, p.wide - p.nlon), jnp.float32)
    for k in (0, p.half):
        scr[k, :, p.nlon : p.nlon + SUB] = jnp.broadcast_to(one, (p.rows, SUB))
        scr[k, :, p.nlon + SUB : p.nlon + 2 * SUB] = jnp.broadcast_to(two, (p.rows, SUB))
    for k in range(p.fields, 2 * p.half):
        scr[k, :, : p.nlon] = jnp.zeros((p.rows, p.nlon), jnp.float32)

    split = p.nlon // (2 * LANES) * LANES
    for move, (t, low, high) in zip(moves, parts):
        move.wait()
        for cols in (slice(0, split), slice(split, p.nlon)):
            acc = [0.0] * (high - low)
            for m in range(p.members):
                f = field[m, :, cols]
                for v in range(low, high):
                    acc[v - low] += held[m, t, v, :, cols].astype(jnp.float32) * f
            for v in range(low, high):
                scr[t * p.vars + v, :, cols] = acc[v - low]

    core = lax.axis_index("mem") % 2
    for k in range(p.half):
        keep[k] = scr[core * p.half + k]
        send[k] = scr[(1 - core) * p.half + k]


def forward(p, perturb, field, hold):
    shape = (p.half, p.rows, p.wide)
    scratch = [
        pltpu.VMEM((2 * p.half, p.rows, p.wide), jnp.float32),
        pltpu.SemaphoreType.DMA((p.slots + 1,)),
    ]
    outs = [jax.ShapeDtypeStruct(shape, jnp.float32)] * 2
    if hold:
        outs = outs + [jax.ShapeDtypeStruct(perturb.shape, perturb.dtype)]
    else:
        scratch = [pltpu.VMEM(perturb.shape, perturb.dtype)] + scratch
    return pl.pallas_call(
        functools.partial(forward_kernel, p),
        in_specs=hbm(1) + vmem(1),
        out_specs=vmem(len(outs)),
        out_shape=outs,
        scratch_shapes=scratch,
        compiler_params=ROOM,
        cost_estimate=cost(p, 2),
        name="forward",
    )(pltpu.with_memory_space_constraint(perturb, pltpu.HBM), field)


def roll(x, shift, axis):
    return pltpu.roll(x, shift % x.shape[axis], axis)


def flip(p, pick, sheet):
    for j in range(p.wide // LANES):
        cols = slice(j * LANES, (j + 1) * LANES)
        tiles = [pick(c, m, cols) for m in range(p.share) for c in range(p.window)]
        if p.used < p.lanes:
            tiles.append(jnp.zeros((p.lanes - p.used, LANES), jnp.float32))
        block = jnp.concatenate(tiles, axis=0)
        for t in range(p.tiles):
            sheet[t, cols, :] = block[t * LANES : (t + 1) * LANES].T


def unflip(p, sheet, out, stop):
    for j in range(-(-stop // LANES)):
        low, high = j * LANES, min((j + 1) * LANES, stop)
        block = [sheet[t, low : low + LANES, :].T for t in range(p.tiles)]
        for m in range(p.share):
            for c in range(p.group):
                at = m * p.run + (p.halo + c) * p.rows
                piece = block[at // LANES][at % LANES : at % LANES + p.rows]
                out[c, m, :, low:high] = piece[:, : high - low]


def lane_row(p):
    lane = lax.broadcasted_iota(jnp.int32, (SUB, p.lanes), 1)
    return lane % p.run, lane


def wrap(p, buf):
    buf[0] = roll(buf[p.step], 1, 0)
    buf[p.step + 1] = roll(buf[1], -1, 0)


def tile(t):
    return slice(t * LANES, (t + 1) * LANES)


def sheet_to(p, sheet, buf):
    def one(i, none):
        for t in range(p.tiles):
            buf[i + 1, :, tile(t)] = sheet[t, pl.ds(i, SUB, stride=p.step), :]
        return none
    lax.fori_loop(0, p.step, one, 0, unroll=p.unroll)


def to_sheet(p, buf, sheet):
    def one(i, none):
        for t in range(p.tiles):
            sheet[t, pl.ds(i, SUB, stride=p.step), :] = buf[i + 1, :, tile(t)]
        return none
    lax.fori_loop(0, p.step, one, 0, unroll=p.unroll)


def one_pass(p, src, dst, east, north, south, diag):
    def body(c, carry):
        f, fw, west = carry
        for k in range(p.stride):
            i = 1 + c * p.stride + k
            fe, here = src[i + 1], east[i]
            across = north[i] * roll(f, -1, 1) + south[i] * roll(f, 1, 1)
            dst[i] = (diag[i] * f + across) + (here * fe + west * fw)
            f, fw, west = fe, f, here
        return f, fw, west
    lax.fori_loop(0, p.step // p.stride, body, (src[1], src[0], east[0]))
    wrap(p, dst)


def ten(p, a, b, *coefs):
    def two(_, none):
        one_pass(p, a, b, *coefs)
        one_pass(p, b, a, *coefs)
        return none
    lax.fori_loop(0, PASSES // 2, two, 0)
    if PASSES % 2:
        one_pass(p, a, b, *coefs)
        a[...] = b[...]


def total_of(p, own, term):
    def one(i, acc):
        return acc + term(i + 1)
    acc = lax.fori_loop(0, p.step, one, jnp.zeros((SUB, p.lanes), jnp.float32), unroll=p.unroll)
    return jnp.sum(jnp.where(own, acc, 0.0))


def own_lanes(p):
    row, lane = lane_row(p)
    first = p.halo * p.rows
    return (row >= first) & (row < first + p.group * p.rows) & (lane < p.used)


def ends(p):
    if p.groups == 1:
        return 0, p.run - 1
    here = lax.axis_index("lat") // p.group * p.group - p.halo
    return jnp.maximum(-here, 0) * p.rows, jnp.minimum(p.lat - here, p.window) * p.rows - 1


def spread(p, low, high, lower, east, north, south, diag):
    row, lane = lane_row(p)

    def coefs(i, none):
        below = lower[i + 1]
        above = jnp.where(row < high, roll(below, -1, 1), 0.0)
        diag[i + 1] = (1.0 - (below + above)) - (east[i + 1] + east[i])
        north[i + 1] = above
        south[i + 1] = jnp.where(row > low, below, 0.0)
        return none
    lax.fori_loop(0, p.step, coefs, 0, unroll=p.unroll)


def first_kernel(p, got, near, far, out, *refs):
    stores, sheet, a, b, north, south, diag, right, east, lower, rows_right, coef, sem = (
        refs[:4], *refs[4:]
    )
    row, lane = lane_row(p)
    low, high = ends(p)
    mine = lax.axis_index("mem") % p.parts
    for k in range(max(p.parts // 2, 1)):
        coef[mine ^ k] = near[k]
    for k in range(p.parts // 2):
        coef[mine ^ (p.parts // 2) ^ k] = far[k]
    per = p.piece // LANES

    def pick(which):
        def of(c, m, cols):
            j = cols.start // LANES
            return coef[j // per, c, which, :, tile(j % per)]
        return of
    flip(p, pick(1), sheet)
    sheet_to(p, sheet, lower)
    flip(p, pick(0), sheet)
    sheet_to(p, sheet, east)
    wrap(p, east)
    inside = (row >= low) & (row <= high) & (lane < p.used)

    def clean(i, none):
        lower[i + 1] = jnp.where(inside, lower[i + 1], 0.0)
        return none
    lax.fori_loop(0, p.step, clean, 0, unroll=p.unroll)
    spread(p, low, high, lower, east, north, south, diag)
    flip(p, lambda c, m, cols: got[c, m, :, cols], sheet)
    sheet_to(p, sheet, a)
    wrap(p, a)
    ten(p, a, b, east, north, south, diag)

    def keep(i, none):
        right[i + 1] = a[i + 1]
        return none
    lax.fori_loop(0, p.step, keep, 0, unroll=p.unroll)
    rr = total_of(p, own_lanes(p), lambda i: a[i] * a[i])
    to_sheet(p, a, sheet)
    unflip(p, sheet, rows_right, p.nlon)
    moves = [
        pltpu.make_async_copy(src, dst, sem.at[k])
        for k, (src, dst) in enumerate(zip((rows_right, right, east, lower), stores))
    ]
    for move in moves:
        move.start()
    ten(p, a, b, east, north, south, diag)
    to_sheet(p, a, sheet)
    sheet[:, p.nlon :, :] = jnp.full((p.tiles, p.wide - p.nlon, LANES), rr)
    unflip(p, sheet, out, p.wide)
    for move in moves:
        move.wait()


def second_kernel(p, got, scal, *refs):
    loads, out, store, ahead, sheet, a, b, north, south, diag, right, east, lower, rows_resid, sem = (
        refs[:3], *refs[3:]
    )
    row, lane = lane_row(p)
    moves = [
        pltpu.make_async_copy(src, dst, sem.at[k])
        for k, (src, dst) in enumerate(zip(loads, (east, lower, right)))
    ]
    for move in moves:
        move.start()
    flip(p, lambda c, m, cols: got[c, m, :, cols], sheet)
    if p.groups == 1:
        q = 0.0
        for t in range(p.tiles):
            first = (row[:1, tile(t)] % p.rows == 0) & (lane[:1, tile(t)] < p.run)
            q = q + jnp.sum(jnp.where(first, sheet[t, p.nlon : p.nlon + 1, :], 0.0))
        q = jnp.full((SUB, LANES), q)
    else:
        q = scal[1][:SUB]
    rr = scal[0][:SUB]
    alpha = rr / (rr + q)
    ahead[...] = alpha
    sheet_to(p, sheet, a)
    wrap(p, a)
    moves[0].wait()
    moves[1].wait()
    spread(p, *ends(p), lower, east, north, south, diag)
    ten(p, a, b, east, north, south, diag)
    moves[2].wait()
    alpha = jnp.broadcast_to(alpha[:, :1], (SUB, p.lanes))

    def cut(i, sums):
        r0 = right[i + 1]
        r = r0 - alpha * (r0 + a[i + 1])
        a[i + 1] = r
        return sums[0] + r * r, sums[1] + r * r0
    zero = jnp.zeros((SUB, p.lanes), jnp.float32)
    rr1, rb = lax.fori_loop(0, p.step, cut, (zero, zero), unroll=p.unroll)
    wrap(p, a)
    own = own_lanes(p)
    rr1 = jnp.sum(jnp.where(own, rr1, 0.0))
    rb = jnp.sum(jnp.where(own, rb, 0.0))
    to_sheet(p, a, sheet)
    unflip(p, sheet, rows_resid, p.nlon)
    leave = pltpu.make_async_copy(rows_resid, store, sem.at[3])
    leave.start()
    ten(p, a, b, east, north, south, diag)
    to_sheet(p, a, sheet)
    sheet[:, p.nlon :, :] = jnp.zeros((p.tiles, p.wide - p.nlon, LANES), jnp.float32)
    sheet[:, p.nlon : p.nlon + SUB, :] = jnp.full((p.tiles, SUB, LANES), rr1)
    sheet[:, p.nlon + SUB : p.nlon + 2 * SUB, :] = jnp.full((p.tiles, SUB, LANES), rb)
    unflip(p, sheet, out, p.wide)
    leave.wait()


def vmem(n):
    return [pl.BlockSpec(memory_space=pltpu.VMEM)] * n


def hbm(n):
    return [pl.BlockSpec(memory_space=pltpu.HBM)] * n


def half_shapes(p):
    buf = (p.step + 2, SUB, p.lanes)
    rows = (p.group, p.share, p.rows, p.nlon)
    back = (p.group, p.share, p.rows, p.wide)
    scratch = [pltpu.VMEM((p.tiles, p.wide, LANES), jnp.float32)]
    scratch += [pltpu.VMEM(buf, jnp.float32)] * 8
    scratch += [pltpu.VMEM(rows, jnp.float32)]
    return *(jax.ShapeDtypeStruct(x, jnp.float32) for x in (buf, rows, back)), scratch


def first_half(p, got, near, far):
    buf, rows, back, scratch = half_shapes(p)
    coef = pltpu.VMEM((p.parts, p.window, 2, p.rows, p.piece), jnp.float32)
    return pl.pallas_call(
        functools.partial(first_kernel, p),
        in_specs=vmem(3),
        out_specs=vmem(1) + hbm(4),
        out_shape=[back] + [pltpu.HBM(x.shape, x.dtype) for x in (rows, buf, buf, buf)],
        scratch_shapes=scratch + [coef, pltpu.SemaphoreType.DMA((4,))],
        compiler_params=ROOM,
        name="smooth_first",
    )(got, near, far)


def second_half(p, got, scal, right, east, lower):
    buf, rows, back, scratch = half_shapes(p)
    return pl.pallas_call(
        functools.partial(second_kernel, p),
        in_specs=vmem(2) + hbm(3),
        out_specs=vmem(1) + hbm(1) + vmem(1),
        out_shape=[
            back,
            pltpu.HBM(rows.shape, rows.dtype),
            jax.ShapeDtypeStruct((SUB, LANES), jnp.float32),
        ],
        scratch_shapes=scratch + [pltpu.SemaphoreType.DMA((4,))],
        compiler_params=ROOM,
        name="smooth_second",
    )(got, scal, *(pltpu.with_memory_space_constraint(x, pltpu.HBM) for x in (east, lower, right)))


def scalars(p, mine, scal):
    rr1 = mine[0, :1, p.nlon : p.nlon + 1]
    rb = mine[0, :1, p.nlon + SUB : p.nlon + SUB + 1]
    rr = scal[0][:1, :1]
    beta = rr1 / rr
    return rr1, beta, rr1 + beta * (2.0 * rb + beta * rr)


def test_kernel(p, weight, total, mine, scal, part):
    at = lax.axis_index("mem") % 2 * p.half
    beta = scalars(p, mine, scal)[1]
    acc = jnp.zeros((p.rows, p.nlon), jnp.float32)
    for k in range(p.half):
        t = mine[k, :, : p.nlon] + beta * total[at + k]
        acc = acc + weight[jnp.minimum(at + k, p.fields - 1)] * t * t
    acc = jnp.broadcast_to(jnp.sum(acc, axis=(0, 1), keepdims=True), part.shape[1:])
    for k in range(part.shape[0]):
        part[k] = acc


def test(p, weight, total, mine, scal):
    copies = 1 if p.groups > 1 else p.mem * p.lat
    return pl.pallas_call(
        functools.partial(test_kernel, p),
        in_specs=vmem(4),
        out_specs=vmem(1)[0],
        out_shape=jax.ShapeDtypeStruct((copies, SUB, LANES), jnp.float32),
        compiler_params=ROOM,
        name="last_sums",
    )(weight, total, mine, scal)


def last_kernel(p, total, mine, other, scal, ahead, q, right, resid, grown, control):
    core = lax.axis_index("mem") % 2
    rr1, beta, length = scalars(p, mine, scal)
    every = q[0]
    for k in range(1, q.shape[0]):
        every = every + q[k]
    every = every[:1, :1] * (2.0 / p.mem)
    step1 = ahead[:1, :1]
    step2 = rr1 / (length + every)
    near = step1 + step2 * beta
    for half, at in ((mine, core * p.half), (other, (1 - core) * p.half)):
        for k in range(p.half):
            @pl.when(at + k < p.fields)
            def _():
                grown[at + k] = near * total[at + k] + step2 * half[k, :, : p.nlon]
    for m in range(p.members):
        control[m] = near * right[m] + step2 * resid[m]


def last(p, total, mine, other, scal, ahead, q, right, resid):
    return pl.pallas_call(
        functools.partial(last_kernel, p),
        in_specs=vmem(8),
        out_specs=vmem(2),
        out_shape=[
            jax.ShapeDtypeStruct((p.fields, p.rows, p.nlon), jnp.float32),
            jax.ShapeDtypeStruct((p.members, p.rows, p.nlon), jnp.float32),
        ],
        compiler_params=ROOM,
        name="last_update",
    )(total, mine, other, scal, ahead, q, right, resid)


def swap(p, x, axis, bit, count):
    return lax.ppermute(x, axis, [(i, i ^ bit) for i in range(count)])


def turn(p, x):
    if p.groups == 1:
        return lax.all_to_all(x, "lat", 0, 0)
    sets = [[g * p.group + i for i in range(p.group)] for g in range(p.groups)]
    return lax.all_to_all(x, "lat", 0, 0, axis_index_groups=sets)


def widen(p, x):
    if p.groups == 1:
        return x
    gap = p.group
    up = [(i, i + gap) for i in range(p.lat - gap)]
    down = [(i + gap, i) for i in range(p.lat - gap)]
    before = lax.ppermute(x[-p.halo :], "lat", up)
    after = lax.ppermute(x[: p.halo], "lat", down)
    return jnp.concatenate([before, x, after], axis=0)


def member_sum(p, keep, send):
    mine = keep + swap(p, send, "mem", 1, p.mem)
    bit = 2
    while bit < p.mem:
        mine = mine + swap(p, mine, "mem", bit, p.mem)
        bit *= 2
    if p.groups > 1:
        tail = lax.psum(mine[:1, :, p.nlon :], "lat") / p.group
        mine = lax.dynamic_update_slice(mine, tail, (0, 0, p.nlon))
    return mine


def coefficients(p, lon_coef, lat_coef):
    both = jnp.pad(jnp.stack([lon_coef, lat_coef]), ((0, 0), (0, 0), (0, p.wide - p.nlon)))
    part = lax.axis_index("mem") % p.parts
    both = lax.dynamic_slice_in_dim(both, part * p.piece, p.piece, axis=2)
    return turn(p, jnp.broadcast_to(both[None], (p.group, 2, p.rows, p.piece)))


def share_out(p, pieces):
    near = widen(p, pieces)[None]
    if p.parts == 1:
        return near, near
    if p.parts == 4:
        near = jnp.concatenate([near, swap(p, near, "mem", 1, p.mem)])
    return near, swap(p, near, "mem", p.parts // 2, p.mem)


def per_device(perturb, innovation, obs_weight, lon_coef, lat_coef):
    p = Plan(perturb, lat_coef, lax.axis_size("mem"), lax.axis_size("lat"))
    flat = lambda x: x.reshape(p.fields, p.rows, p.nlon)
    by_rank = lambda x: x.reshape((p.members,) + x.shape[2:])
    weight = flat(obs_weight)
    by_member = perturb.reshape(p.members, p.fields, p.rows, p.nlon)

    pieces = coefficients(p, lon_coef, lat_coef)
    sent = adjoint_first(p, by_member, weight, flat(innovation))
    near, far = share_out(p, pieces)
    back, rows_right, *kept = first_half(p, widen(p, turn(p, sent)), near, far)
    field, rows_right = lax.optimization_barrier((turn(p, back), rows_right))
    with jax.named_scope("return_first"):
        rows_right = by_rank(turn(p, rows_right))
    with jax.named_scope("map_first"):
        keep, send, held = forward(p, perturb, by_rank(field), True)
    mine = member_sum(p, keep, send)
    other = swap(p, mine, "mem", 1, p.mem)
    sent, total, scal = adjoint(p, held.reshape(by_member.shape), weight, mine, other)
    sent, rows_right = lax.optimization_barrier((sent, rows_right))
    if p.groups > 1:
        scal = jnp.concatenate([scal[:1], lax.psum(scal[1:], "lat")], axis=0)
    back, rows_resid, ahead = second_half(p, widen(p, turn(p, sent)), scal, *kept)
    field, rows_resid = lax.optimization_barrier((turn(p, back), rows_resid))
    with jax.named_scope("return_second"):
        rows_resid = by_rank(turn(p, rows_resid))
    with jax.named_scope("map_second"):
        keep, send = forward(p, perturb, by_rank(field), False)
    mine = member_sum(p, keep, send)
    mine, rows_resid = lax.optimization_barrier((mine, rows_resid))
    other = swap(p, mine, "mem", 1, p.mem)
    q = test(p, weight, total, mine, scal)
    q = lax.all_to_all(q, ("mem", "lat"), 0, 0) if p.groups == 1 else lax.psum(q, ("mem", "lat"))
    grown, control = last(p, total, mine, other, scal, ahead, q, rows_right, rows_resid)
    return control, grown.reshape(p.slots, p.vars, p.rows, p.nlon)


def solution(mesh):
    return jax.shard_map(
        per_device,
        mesh=mesh,
        in_specs=(
            P("mem", None, None, "lat", None),
            P(None, None, "lat", None),
            P(None, None, "lat", None),
            P("lat", None),
            P("lat", None),
        ),
        out_specs=(P("mem", "lat", None), P(None, None, "lat", None)),
        check_vma=False,
    )
```

```python
import functools

import jax
import jax.numpy as jnp
from jax import lax
from jax.experimental import pallas as pl
from jax.experimental.pallas import tpu as pltpu
from jax.sharding import PartitionSpec as P


PASSES = 10
LANES = 128
SUB = 8
ROOM = pltpu.CompilerParams(vmem_limit_bytes=24 * 2**20)


def ceil_to(value, unit):
    return -(-value // unit) * unit


class Plan:
    def __init__(self, perturb, mem, lat):
        self.members, self.slots, self.vars, self.rows, self.nlon = perturb.shape
        self.mem, self.lat = mem, lat
        self.fields = self.slots * self.vars
        self.half = (self.fields + 2) // 2
        self.wide = ceil_to(self.nlon + 16, LANES)
        halo = -(-2 * PASSES // self.rows)
        self.group = max(
            g for g in range(1, lat + 1)
            if lat % g == 0 and self.members % g == 0 and (g == lat or g >= halo)
        )
        self.groups = lat // self.group
        self.halo = 0 if self.groups == 1 else halo
        self.share = self.members // self.group
        self.window = self.group + 2 * self.halo
        self.run = self.window * self.rows
        self.used = self.share * self.run
        self.lanes = ceil_to(self.used, LANES)
        self.tiles = self.lanes // LANES
        self.step = self.nlon // SUB
        self.unroll = max(u for u in range(1, 21) if self.step % u == 0)
        self.stride = max(u for u in range(1, 181) if self.step % u == 0)
        self.parts = max(
            q for q in (1, 2, 4) if mem % q == 0 and self.wide % (q * LANES) == 0
        )
        self.piece = self.wide // self.parts
        self.doubling = self.groups == 1 and lat > 1 and lat & (lat - 1) == 0


def mapped(p, perturb, first, prod):
    acc = [0.0] * p.share
    for k in range(p.fields):
        row = prod[k]
        for m in range(p.share):
            acc[m] = acc[m] + perturb[first + m, k].astype(jnp.float32) * row
    return acc


def adjoint_first_kernel(p, perturb, weight, value, out, pbuf, wbuf, vbuf, obuf, prod, sem):
    def part(k):
        rows = pl.ds(k * p.share, p.share)
        return pltpu.make_async_copy(perturb.at[rows], pbuf.at[rows], sem.at[k])

    def leave(k):
        return pltpu.make_async_copy(obuf.at[k], out.at[k], sem.at[p.group + k])

    heads = [
        pltpu.make_async_copy(weight, wbuf, sem.at[2 * p.group]),
        pltpu.make_async_copy(value, vbuf, sem.at[2 * p.group + 1]),
    ]
    for head in heads:
        head.start()
    for k in range(p.group):
        part(k).start()
    for head in heads:
        head.wait()
    for k in range(p.fields):
        prod[k] = wbuf[k] * vbuf[k]

    def one(k, none):
        part(k).wait()
        acc = mapped(p, pbuf, k * p.share, prod)
        for m in range(p.share):
            obuf[k, m, :, : p.nlon] = acc[m]
            obuf[k, m, :, p.nlon :] = jnp.zeros((p.rows, p.wide - p.nlon), jnp.float32)
        leave(k).start()
        return none
    lax.fori_loop(0, p.group, one, 0)
    for k in range(p.group):
        leave(k).wait()


def adjoint_first(p, perturb, weight, value):
    shape = (p.group, p.share, p.rows, p.wide)
    field = pltpu.VMEM((p.fields, p.rows, p.nlon), jnp.float32)
    held = [pltpu.with_memory_space_constraint(x, pltpu.HBM) for x in (perturb, weight, value)]
    return pl.pallas_call(
        functools.partial(adjoint_first_kernel, p),
        in_specs=hbm(3),
        out_specs=hbm(1)[0],
        out_shape=pltpu.HBM(shape, jnp.float32),
        scratch_shapes=[
            pltpu.VMEM(perturb.shape, perturb.dtype),
            field,
            field,
            pltpu.VMEM(shape, jnp.float32),
            field,
            pltpu.SemaphoreType.DMA((2 * p.group + 2,)),
        ],
        compiler_params=ROOM,
        cost_estimate=cost(p, 2),
        name="adjoint_first",
    )(*held)


def adjoint_kernel(p, perturb, weight, mine, other, out, total, scal, prod):
    step = pl.program_id(0)

    @pl.when(step == 0)
    def _():
        core = lax.axis_index("mem") % 2
        acc = jnp.zeros((p.rows, p.nlon), jnp.float32)
        for half, at in ((mine, core * p.half), (other, (1 - core) * p.half)):
            for k in range(p.half):
                t = half[k, :, : p.nlon]
                wt = weight[jnp.minimum(at + k, p.fields - 1)] * t
                prod[at + k] = wt
                total[at + k] = t
                acc = acc + wt * t
        rr = mine[0, :1, p.nlon : p.nlon + 1]
        scal[0] = jnp.broadcast_to(rr, (p.rows, LANES))
        scal[1] = jnp.full((p.rows, LANES), jnp.sum(acc))

    acc = mapped(p, perturb, 0, prod)
    tail = jnp.broadcast_to(scal[1][:1, :1], (p.rows, p.wide - p.nlon))
    for m in range(p.share):
        out[0, m, :, : p.nlon] = acc[m]
        out[0, m, :, p.nlon :] = tail


def adjoint(p, perturb, weight, mine, other):
    whole = lambda *shape: pl.BlockSpec(shape, lambda i: (0,) * len(shape))
    rows, nlon = p.rows, p.nlon
    return pl.pallas_call(
        functools.partial(adjoint_kernel, p),
        grid=(p.group,),
        in_specs=[
            pl.BlockSpec((p.share, p.fields, rows, nlon), lambda i: (i, 0, 0, 0)),
            whole(p.fields, rows, nlon),
            whole(p.half, rows, p.wide),
            whole(p.half, rows, p.wide),
        ],
        out_specs=[
            pl.BlockSpec((1, p.share, rows, p.wide), lambda i: (i, 0, 0, 0)),
            whole(2 * p.half, rows, nlon),
            whole(2, rows, LANES),
        ],
        out_shape=[
            jax.ShapeDtypeStruct((p.group, p.share, rows, p.wide), jnp.float32),
            jax.ShapeDtypeStruct((2 * p.half, rows, nlon), jnp.float32),
            jax.ShapeDtypeStruct((2, rows, LANES), jnp.float32),
        ],
        scratch_shapes=[pltpu.VMEM((2 * p.half, rows, nlon), jnp.float32)],
        compiler_params=ROOM,
        cost_estimate=cost(p, 2),
        name="adjoint_second",
    )(perturb, weight, mine, other)


def cost(p, size):
    cells = p.members * p.fields * p.rows * p.nlon
    return pl.CostEstimate(flops=2 * cells, bytes_accessed=size * cells, transcendentals=0)


def forward_kernel(p, perturb, field, keep, send, held, scr, sem):
    cut = -(-p.vars // 2)
    parts = [(t, 0, p.vars) for t in range(p.slots - 1)]
    parts += [(p.slots - 1, 0, cut), (p.slots - 1, cut, p.vars)]
    moves = []
    for n, (t, low, high) in enumerate(parts):
        at = (slice(None), t, pl.ds(low, high - low))
        moves.append(pltpu.make_async_copy(perturb.at[at], held.at[at], sem.at[n]))
        moves[-1].start()

    one = jnp.zeros((1, 1), jnp.float32)
    two = jnp.zeros((1, 1), jnp.float32)
    for k in range(p.group):
        one = one + field[k * p.share, :1, p.nlon : p.nlon + 1]
        two = two + field[k * p.share, :1, p.nlon + SUB : p.nlon + SUB + 1]
    for k in range(2 * p.half):
        scr[k, :, p.nlon :] = jnp.zeros((p.rows, p.wide - p.nlon), jnp.float32)
    for k in (0, p.half):
        scr[k, :, p.nlon : p.nlon + SUB] = jnp.broadcast_to(one, (p.rows, SUB))
        scr[k, :, p.nlon + SUB : p.nlon + 2 * SUB] = jnp.broadcast_to(two, (p.rows, SUB))
    for k in range(p.fields, 2 * p.half):
        scr[k, :, : p.nlon] = jnp.zeros((p.rows, p.nlon), jnp.float32)

    split = p.nlon // (2 * LANES) * LANES
    for move, (t, low, high) in zip(moves, parts):
        move.wait()
        for cols in (slice(0, split), slice(split, p.nlon)):
            acc = [0.0] * (high - low)
            for m in range(p.members):
                f = field[m, :, cols]
                for v in range(low, high):
                    acc[v - low] += held[m, t, v, :, cols].astype(jnp.float32) * f
            for v in range(low, high):
                scr[t * p.vars + v, :, cols] = acc[v - low]

    core = lax.axis_index("mem") % 2
    for k in range(p.half):
        keep[k] = scr[core * p.half + k]
        send[k] = scr[(1 - core) * p.half + k]


def forward(p, perturb, field, hold):
    shape = (p.half, p.rows, p.wide)
    scratch = [
        pltpu.VMEM((2 * p.half, p.rows, p.wide), jnp.float32),
        pltpu.SemaphoreType.DMA((p.slots + 1,)),
    ]
    outs = [jax.ShapeDtypeStruct(shape, jnp.float32)] * 2
    if hold:
        outs = outs + [jax.ShapeDtypeStruct(perturb.shape, perturb.dtype)]
    else:
        scratch = [pltpu.VMEM(perturb.shape, perturb.dtype)] + scratch
    return pl.pallas_call(
        functools.partial(forward_kernel, p),
        in_specs=hbm(1) + vmem(1),
        out_specs=vmem(len(outs)),
        out_shape=outs,
        scratch_shapes=scratch,
        compiler_params=ROOM,
        cost_estimate=cost(p, 2),
        name="forward",
    )(pltpu.with_memory_space_constraint(perturb, pltpu.HBM), field)


def roll(x, shift, axis):
    return pltpu.roll(x, shift % x.shape[axis], axis)


def flip(p, pick, sheet):
    for j in range(p.wide // LANES):
        cols = slice(j * LANES, (j + 1) * LANES)
        tiles = [pick(c, m, cols) for m in range(p.share) for c in range(p.window)]
        if p.used < p.lanes:
            tiles.append(jnp.zeros((p.lanes - p.used, LANES), jnp.float32))
        block = jnp.concatenate(tiles, axis=0)
        for t in range(p.tiles):
            sheet[t, cols, :] = block[t * LANES : (t + 1) * LANES].T


def unflip(p, sheet, out, stop):
    for j in range(-(-stop // LANES)):
        low, high = j * LANES, min((j + 1) * LANES, stop)
        block = [sheet[t, low : low + LANES, :].T for t in range(p.tiles)]
        for m in range(p.share):
            for c in range(p.group):
                at = m * p.run + (p.halo + c) * p.rows
                piece = block[at // LANES][at % LANES : at % LANES + p.rows]
                out[c, m, :, low:high] = piece[:, : high - low]


def lane_row(p):
    lane = lax.broadcasted_iota(jnp.int32, (SUB, p.lanes), 1)
    return lane % p.run, lane


def wrap(p, buf):
    buf[0] = roll(buf[p.step], 1, 0)
    buf[p.step + 1] = roll(buf[1], -1, 0)


def tile(t):
    return slice(t * LANES, (t + 1) * LANES)


def sheet_to(p, sheet, buf):
    def one(i, none):
        for t in range(p.tiles):
            buf[i + 1, :, tile(t)] = sheet[t, pl.ds(i, SUB, stride=p.step), :]
        return none
    lax.fori_loop(0, p.step, one, 0, unroll=p.unroll)


def to_sheet(p, buf, sheet):
    def one(i, none):
        for t in range(p.tiles):
            sheet[t, pl.ds(i, SUB, stride=p.step), :] = buf[i + 1, :, tile(t)]
        return none
    lax.fori_loop(0, p.step, one, 0, unroll=p.unroll)


def one_pass(p, src, dst, east, north, south, diag):
    def body(c, carry):
        f, fw, west = carry
        for k in range(p.stride):
            i = 1 + c * p.stride + k
            fe, here = src[i + 1], east[i]
            across = north[i] * roll(f, -1, 1) + south[i] * roll(f, 1, 1)
            dst[i] = (diag[i] * f + across) + (here * fe + west * fw)
            f, fw, west = fe, f, here
        return f, fw, west
    lax.fori_loop(0, p.step // p.stride, body, (src[1], src[0], east[0]))
    wrap(p, dst)


def ten(p, a, b, *coefs):
    def two(_, none):
        one_pass(p, a, b, *coefs)
        one_pass(p, b, a, *coefs)
        return none
    lax.fori_loop(0, PASSES // 2, two, 0)
    if PASSES % 2:
        one_pass(p, a, b, *coefs)
        a[...] = b[...]


def total_of(p, own, term):
    def one(i, acc):
        return acc + term(i + 1)
    acc = lax.fori_loop(0, p.step, one, jnp.zeros((SUB, p.lanes), jnp.float32), unroll=p.unroll)
    return jnp.sum(jnp.where(own, acc, 0.0))


def own_lanes(p):
    row, lane = lane_row(p)
    first = p.halo * p.rows
    return (row >= first) & (row < first + p.group * p.rows) & (lane < p.used)


def ends(p):
    if p.groups == 1:
        return 0, p.run - 1
    here = lax.axis_index("lat") // p.group * p.group - p.halo
    return jnp.maximum(-here, 0) * p.rows, jnp.minimum(p.lat - here, p.window) * p.rows - 1


def spread(p, low, high, lower, east, north, south, diag):
    row, _ = lane_row(p)

    def coefs(i, none):
        below = lower[i + 1]
        above = jnp.where(row < high, roll(below, -1, 1), 0.0)
        diag[i + 1] = (1.0 - (below + above)) - (east[i + 1] + east[i])
        north[i + 1] = above
        south[i + 1] = jnp.where(row > low, below, 0.0)
        return none
    lax.fori_loop(0, p.step, coefs, 0, unroll=p.unroll)


def first_kernel(p, got, near, far, out, *refs):
    stores, sheet, a, b, north, south, diag, right, east, lower, rows_right, coef, sem = (
        refs[:4], *refs[4:]
    )
    row, lane = lane_row(p)
    low, high = ends(p)
    mine = lax.axis_index("mem") % p.parts
    here = lax.axis_index("lat") if p.doubling else 0
    for c in range(p.window):
        for k in range(max(p.parts // 2, 1)):
            coef[mine ^ k, here ^ c] = near[k, c]
        for k in range(p.parts // 2):
            coef[mine ^ (p.parts // 2) ^ k, here ^ c] = far[k, c]
    per = p.piece // LANES

    def pick(which):
        def of(c, m, cols):
            j = cols.start // LANES
            return coef[j // per, c, which, :, tile(j % per)]
        return of
    flip(p, pick(1), sheet)
    sheet_to(p, sheet, lower)
    flip(p, pick(0), sheet)
    sheet_to(p, sheet, east)
    wrap(p, east)
    inside = (row >= low) & (row <= high) & (lane < p.used)

    def clean(i, none):
        lower[i + 1] = jnp.where(inside, lower[i + 1], 0.0)
        return none
    lax.fori_loop(0, p.step, clean, 0, unroll=p.unroll)
    spread(p, low, high, lower, east, north, south, diag)
    flip(p, lambda c, m, cols: got[c, m, :, cols], sheet)
    sheet_to(p, sheet, a)
    wrap(p, a)
    ten(p, a, b, east, north, south, diag)

    def keep(i, none):
        right[i + 1] = a[i + 1]
        return none
    lax.fori_loop(0, p.step, keep, 0, unroll=p.unroll)
    rr = total_of(p, own_lanes(p), lambda i: a[i] * a[i])
    to_sheet(p, a, sheet)
    unflip(p, sheet, rows_right, p.nlon)
    moves = [
        pltpu.make_async_copy(src, dst, sem.at[k])
        for k, (src, dst) in enumerate(zip((rows_right, right, east, lower), stores))
    ]
    for move in moves:
        move.start()
    ten(p, a, b, east, north, south, diag)
    to_sheet(p, a, sheet)
    sheet[:, p.nlon :, :] = jnp.full((p.tiles, p.wide - p.nlon, LANES), rr)
    unflip(p, sheet, out, p.wide)
    for move in moves:
        move.wait()


def second_kernel(p, got, scal, *refs):
    loads, out, store, ahead, sheet, a, b, north, south, diag, right, east, lower, rows_resid, sem = (
        refs[:3], *refs[3:]
    )
    row, lane = lane_row(p)
    moves = [
        pltpu.make_async_copy(src, dst, sem.at[k])
        for k, (src, dst) in enumerate(zip(loads, (east, lower, right)))
    ]
    for move in moves:
        move.start()
    flip(p, lambda c, m, cols: got[c, m, :, cols], sheet)
    if p.groups == 1:
        q = 0.0
        for t in range(p.tiles):
            first = (row[:1, tile(t)] % p.rows == 0) & (lane[:1, tile(t)] < p.run)
            q = q + jnp.sum(jnp.where(first, sheet[t, p.nlon : p.nlon + 1, :], 0.0))
        q = jnp.full((SUB, LANES), q)
    else:
        q = scal[1][:SUB]
    rr = scal[0][:SUB]
    alpha = rr / (rr + q)
    ahead[...] = alpha
    sheet_to(p, sheet, a)
    wrap(p, a)
    moves[0].wait()
    moves[1].wait()
    spread(p, *ends(p), lower, east, north, south, diag)
    ten(p, a, b, east, north, south, diag)
    moves[2].wait()
    alpha = jnp.broadcast_to(alpha[:, :1], (SUB, p.lanes))

    def cut(i, sums):
        r0 = right[i + 1]
        r = r0 - alpha * (r0 + a[i + 1])
        a[i + 1] = r
        return sums[0] + r * r, sums[1] + r * r0
    zero = jnp.zeros((SUB, p.lanes), jnp.float32)
    rr1, rb = lax.fori_loop(0, p.step, cut, (zero, zero), unroll=p.unroll)
    wrap(p, a)
    own = own_lanes(p)
    rr1 = jnp.sum(jnp.where(own, rr1, 0.0))
    rb = jnp.sum(jnp.where(own, rb, 0.0))
    to_sheet(p, a, sheet)
    unflip(p, sheet, rows_resid, p.nlon)
    leave = pltpu.make_async_copy(rows_resid, store, sem.at[3])
    leave.start()
    ten(p, a, b, east, north, south, diag)
    to_sheet(p, a, sheet)
    sheet[:, p.nlon :, :] = jnp.zeros((p.tiles, p.wide - p.nlon, LANES), jnp.float32)
    sheet[:, p.nlon : p.nlon + SUB, :] = jnp.full((p.tiles, SUB, LANES), rr1)
    sheet[:, p.nlon + SUB : p.nlon + 2 * SUB, :] = jnp.full((p.tiles, SUB, LANES), rb)
    unflip(p, sheet, out, p.wide)
    leave.wait()


def vmem(n):
    return [pl.BlockSpec(memory_space=pltpu.VMEM)] * n


def hbm(n):
    return [pl.BlockSpec(memory_space=pltpu.HBM)] * n


def half_shapes(p):
    buf = (p.step + 2, SUB, p.lanes)
    rows = (p.group, p.share, p.rows, p.nlon)
    back = (p.group, p.share, p.rows, p.wide)
    scratch = [pltpu.VMEM((p.tiles, p.wide, LANES), jnp.float32)]
    scratch += [pltpu.VMEM(buf, jnp.float32)] * 8
    scratch += [pltpu.VMEM(rows, jnp.float32)]
    return *(jax.ShapeDtypeStruct(x, jnp.float32) for x in (buf, rows, back)), scratch


def first_half(p, got, near, far):
    buf, rows, back, scratch = half_shapes(p)
    coef = pltpu.VMEM((p.parts, p.window, 2, p.rows, p.piece), jnp.float32)
    return pl.pallas_call(
        functools.partial(first_kernel, p),
        in_specs=vmem(3),
        out_specs=vmem(1) + hbm(4),
        out_shape=[back] + [pltpu.HBM(x.shape, x.dtype) for x in (rows, buf, buf, buf)],
        scratch_shapes=scratch + [coef, pltpu.SemaphoreType.DMA((4,))],
        compiler_params=ROOM,
        name="smooth_first",
    )(got, near, far)


def second_half(p, got, scal, right, east, lower):
    _, rows, back, scratch = half_shapes(p)
    return pl.pallas_call(
        functools.partial(second_kernel, p),
        in_specs=vmem(2) + hbm(3),
        out_specs=vmem(1) + hbm(1) + vmem(1),
        out_shape=[
            back,
            pltpu.HBM(rows.shape, rows.dtype),
            jax.ShapeDtypeStruct((SUB, LANES), jnp.float32),
        ],
        scratch_shapes=scratch + [pltpu.SemaphoreType.DMA((4,))],
        compiler_params=ROOM,
        name="smooth_second",
    )(got, scal, *(pltpu.with_memory_space_constraint(x, pltpu.HBM) for x in (east, lower, right)))


def scalars(p, mine, scal):
    rr1 = mine[0, :1, p.nlon : p.nlon + 1]
    rb = mine[0, :1, p.nlon + SUB : p.nlon + SUB + 1]
    rr = scal[0][:1, :1]
    beta = rr1 / rr
    return rr1, beta, rr1 + beta * (2.0 * rb + beta * rr)


def test_kernel(p, weight, total, mine, scal, part):
    at = lax.axis_index("mem") % 2 * p.half
    beta = scalars(p, mine, scal)[1]
    acc = jnp.zeros((p.rows, p.nlon), jnp.float32)
    for k in range(p.half):
        t = mine[k, :, : p.nlon] + beta * total[at + k]
        acc = acc + weight[jnp.minimum(at + k, p.fields - 1)] * t * t
    acc = jnp.broadcast_to(jnp.sum(acc, axis=(0, 1), keepdims=True), part.shape[1:])
    for k in range(part.shape[0]):
        part[k] = acc


def test(p, weight, total, mine, scal):
    copies = 1 if p.groups > 1 else p.mem * p.lat
    return pl.pallas_call(
        functools.partial(test_kernel, p),
        in_specs=vmem(4),
        out_specs=vmem(1)[0],
        out_shape=jax.ShapeDtypeStruct((copies, SUB, LANES), jnp.float32),
        compiler_params=ROOM,
        name="last_sums",
    )(weight, total, mine, scal)


def last_kernel(p, total, mine, other, scal, ahead, q, right, resid, grown, control):
    core = lax.axis_index("mem") % 2
    rr1, beta, length = scalars(p, mine, scal)
    every = q[0]
    for k in range(1, q.shape[0]):
        every = every + q[k]
    every = every[:1, :1] * (2.0 / p.mem)
    step1 = ahead[:1, :1]
    step2 = rr1 / (length + every)
    near = step1 + step2 * beta
    for half, at in ((mine, core * p.half), (other, (1 - core) * p.half)):
        for k in range(p.half):
            @pl.when(at + k < p.fields)
            def _():
                grown[at + k] = near * total[at + k] + step2 * half[k, :, : p.nlon]
    for m in range(p.members):
        control[m] = near * right[m] + step2 * resid[m]


def last(p, total, mine, other, scal, ahead, q, right, resid):
    return pl.pallas_call(
        functools.partial(last_kernel, p),
        in_specs=vmem(8),
        out_specs=vmem(2),
        out_shape=[
            jax.ShapeDtypeStruct((p.fields, p.rows, p.nlon), jnp.float32),
            jax.ShapeDtypeStruct((p.members, p.rows, p.nlon), jnp.float32),
        ],
        compiler_params=ROOM,
        name="last_update",
    )(total, mine, other, scal, ahead, q, right, resid)


def swap(x, axis, bit, count):
    return lax.ppermute(x, axis, [(i, i ^ bit) for i in range(count)])


def turn(p, x):
    if p.groups == 1:
        return lax.all_to_all(x, "lat", 0, 0)
    sets = [[g * p.group + i for i in range(p.group)] for g in range(p.groups)]
    return lax.all_to_all(x, "lat", 0, 0, axis_index_groups=sets)


def widen(p, x):
    if p.groups == 1:
        return x
    gap = p.group
    up = [(i, i + gap) for i in range(p.lat - gap)]
    down = [(i + gap, i) for i in range(p.lat - gap)]
    before = lax.ppermute(x[-p.halo :], "lat", up)
    after = lax.ppermute(x[: p.halo], "lat", down)
    return jnp.concatenate([before, x, after], axis=0)


def member_sum(p, keep, send):
    mine = keep + swap(send, "mem", 1, p.mem)
    bit = 2
    while bit < p.mem:
        mine = mine + swap(mine, "mem", bit, p.mem)
        bit *= 2
    if p.groups > 1:
        tail = lax.psum(mine[:1, :, p.nlon :], "lat") / p.group
        mine = lax.dynamic_update_slice(mine, tail, (0, 0, p.nlon))
    return mine


def coefficients(p, lon_coef, lat_coef):
    both = jnp.pad(jnp.stack([lon_coef, lat_coef]), ((0, 0), (0, 0), (0, p.wide - p.nlon)))
    part = lax.axis_index("mem") % p.parts
    both = lax.dynamic_slice_in_dim(both, part * p.piece, p.piece, axis=2)[None]
    if not p.doubling:
        return turn(p, jnp.broadcast_to(both, (p.group, 2, p.rows, p.piece)))
    return jnp.concatenate([both, swap(both, "lat", 1, p.lat)])


def gather_on(p, pieces):
    bit = 2
    while p.doubling and bit < p.lat:
        pieces = jnp.concatenate([pieces, swap(pieces, "lat", bit, p.lat)])
        bit *= 2
    return pieces


def share_out(p, pieces):
    near = widen(p, gather_on(p, pieces))[None]
    if p.parts == 1:
        return near, near
    if p.parts == 4:
        near = jnp.concatenate([near, swap(near, "mem", 1, p.mem)])
    return near, swap(near, "mem", p.parts // 2, p.mem)


def per_device(perturb, innovation, obs_weight, lon_coef, lat_coef):
    p = Plan(perturb, lax.axis_size("mem"), lax.axis_size("lat"))
    flat = lambda x: x.reshape(p.fields, p.rows, p.nlon)
    by_rank = lambda x: x.reshape((p.members,) + x.shape[2:])
    weight = flat(obs_weight)
    by_member = perturb.reshape(p.members, p.fields, p.rows, p.nlon)

    pieces = coefficients(p, lon_coef, lat_coef)
    sent = adjoint_first(p, by_member, weight, flat(innovation))
    if p.doubling:
        sent, pieces = lax.optimization_barrier((sent, pieces))
    got = turn(p, sent)
    near, far = share_out(p, pieces)
    back, rows_right, *kept = first_half(p, widen(p, got), near, far)
    field, rows_right = lax.optimization_barrier((turn(p, back), rows_right))
    rows_right = by_rank(turn(p, rows_right))
    keep, send, held = forward(p, perturb, by_rank(field), True)
    mine = member_sum(p, keep, send)
    other = swap(mine, "mem", 1, p.mem)
    sent, total, scal = adjoint(p, held.reshape(by_member.shape), weight, mine, other)
    sent, rows_right = lax.optimization_barrier((sent, rows_right))
    if p.groups > 1:
        scal = jnp.concatenate([scal[:1], lax.psum(scal[1:], "lat")], axis=0)
    back, rows_resid, ahead = second_half(p, widen(p, turn(p, sent)), scal, *kept)
    field, rows_resid = lax.optimization_barrier((turn(p, back), rows_resid))
    rows_resid = by_rank(turn(p, rows_resid))
    keep, send = forward(p, perturb, by_rank(field), False)
    mine = member_sum(p, keep, send)
    mine, rows_resid = lax.optimization_barrier((mine, rows_resid))
    other = swap(mine, "mem", 1, p.mem)
    q = test(p, weight, total, mine, scal)
    q = lax.all_to_all(q, ("mem", "lat"), 0, 0) if p.groups == 1 else lax.psum(q, ("mem", "lat"))
    grown, control = last(p, total, mine, other, scal, ahead, q, rows_right, rows_resid)
    return control, grown.reshape(p.slots, p.vars, p.rows, p.nlon)


def solution(mesh):
    return jax.shard_map(
        per_device,
        mesh=mesh,
        in_specs=(
            P("mem", None, None, "lat", None),
            P(None, None, "lat", None),
            P(None, None, "lat", None),
            P("lat", None),
            P("lat", None),
        ),
        out_specs=(P("mem", "lat", None), P(None, None, "lat", None)),
        check_vma=False,
    )
```

```python
import functools

import jax
import jax.numpy as jnp
from jax import lax
from jax.experimental import pallas as pl
from jax.experimental.pallas import tpu as pltpu
from jax.sharding import PartitionSpec as P

PASSES = 10
LANES = 128
SUB = 8
ROOM = pltpu.CompilerParams(vmem_limit_bytes=24 * 2**20)


def ceil_to(value, unit):
    return -(-value // unit) * unit


class Plan:
    def __init__(self, perturb, lat_coef, mem, lat):
        self.members, self.slots, self.vars, self.rows, self.nlon = perturb.shape
        self.mem, self.lat = mem, lat
        self.fields = self.slots * self.vars
        self.half = (self.fields + 2) // 2
        self.wide = ceil_to(self.nlon + 16, LANES)
        halo = -(-2 * PASSES // self.rows)
        self.group = max(
            g for g in range(1, lat + 1)
            if lat % g == 0 and self.members % g == 0 and (g == lat or g >= halo)
        )
        self.groups = lat // self.group
        self.halo = 0 if self.groups == 1 else halo
        self.share = self.members // self.group
        self.window = self.group + 2 * self.halo
        self.run = self.window * self.rows
        self.used = self.share * self.run
        self.lanes = ceil_to(self.used, LANES)
        self.tiles = self.lanes // LANES
        self.step = self.nlon // SUB
        self.unroll = self.stride = max(u for u in range(1, 181) if self.step % u == 0)
        self.parts = max(
            q for q in (1, 2, 4) if mem % q == 0 and self.wide % (q * LANES) == 0
        )
        self.piece = self.wide // self.parts


def mapped(p, perturb, first, prod):
    acc = [0.0] * p.share
    for k in range(p.fields):
        row = prod[k]
        for m in range(p.share):
            acc[m] = acc[m] + perturb[first + m, k].astype(jnp.float32) * row
    return acc


def adjoint_first_kernel(p, perturb, weight, value, out, pbuf, wbuf, vbuf, obuf, prod, sem):
    def part(k):
        rows = pl.ds(k * p.share, p.share)
        return pltpu.make_async_copy(perturb.at[rows], pbuf.at[rows], sem.at[k])

    def leave(k):
        return pltpu.make_async_copy(obuf.at[k], out.at[k], sem.at[p.group + k])

    heads = [
        pltpu.make_async_copy(weight, wbuf, sem.at[2 * p.group]),
        pltpu.make_async_copy(value, vbuf, sem.at[2 * p.group + 1]),
    ]
    for head in heads:
        head.start()
    for k in range(p.group):
        part(k).start()
    for head in heads:
        head.wait()
    for k in range(p.fields):
        prod[k] = wbuf[k] * vbuf[k]

    def one(k, none):
        part(k).wait()
        acc = mapped(p, pbuf, k * p.share, prod)
        for m in range(p.share):
            obuf[k, m, :, : p.nlon] = acc[m]
            obuf[k, m, :, p.nlon :] = jnp.zeros((p.rows, p.wide - p.nlon), jnp.float32)
        leave(k).start()
        return none
    lax.fori_loop(0, p.group, one, 0)
    for k in range(p.group):
        leave(k).wait()


def adjoint_first(p, perturb, weight, value):
    shape = (p.group, p.share, p.rows, p.wide)
    field = pltpu.VMEM((p.fields, p.rows, p.nlon), jnp.float32)
    held = [pltpu.with_memory_space_constraint(x, pltpu.HBM) for x in (perturb, weight, value)]
    return pl.pallas_call(
        functools.partial(adjoint_first_kernel, p),
        in_specs=hbm(3),
        out_specs=hbm(1)[0],
        out_shape=pltpu.HBM(shape, jnp.float32),
        scratch_shapes=[
            pltpu.VMEM(perturb.shape, perturb.dtype),
            field,
            field,
            pltpu.VMEM(shape, jnp.float32),
            field,
            pltpu.SemaphoreType.DMA((2 * p.group + 2,)),
        ],
        compiler_params=ROOM,
        cost_estimate=cost(p, 2),
        name="adjoint_first",
    )(*held)


def adjoint_kernel(p, perturb, weight, mine, other, out, store, scal, prod, total, sem):
    step = pl.program_id(0)
    leave = pltpu.make_async_copy(total, store, sem)

    @pl.when(step == 0)
    def _():
        core = lax.axis_index("mem") % 2
        acc = jnp.zeros((p.rows, p.nlon), jnp.float32)
        for half, at in ((mine, core * p.half), (other, (1 - core) * p.half)):
            for k in range(p.half):
                t = half[k, :, : p.nlon]
                wt = weight[jnp.minimum(at + k, p.fields - 1)] * t
                prod[at + k] = wt
                total[at + k] = t
                acc = acc + wt * t
        rr = mine[0, :1, p.nlon : p.nlon + 1]
        scal[0] = jnp.broadcast_to(rr, (p.rows, LANES))
        scal[1] = jnp.full((p.rows, LANES), jnp.sum(acc))
        leave.start()

    acc = mapped(p, perturb, 0, prod)
    tail = jnp.broadcast_to(scal[1][:1, :1], (p.rows, p.wide - p.nlon))
    for m in range(p.share):
        out[0, m, :, : p.nlon] = acc[m]
        out[0, m, :, p.nlon :] = tail

    @pl.when(step == p.group - 1)
    def _():
        leave.wait()


def adjoint(p, perturb, weight, mine, other):
    whole = lambda *shape: pl.BlockSpec(shape, lambda i: (0,) * len(shape))
    rows, nlon = p.rows, p.nlon
    return pl.pallas_call(
        functools.partial(adjoint_kernel, p),
        grid=(p.group,),
        in_specs=[
            pl.BlockSpec((p.share, p.fields, rows, nlon), lambda i: (i, 0, 0, 0)),
            whole(p.fields, rows, nlon),
            whole(p.half, rows, p.wide),
            whole(p.half, rows, p.wide),
        ],
        out_specs=[
            pl.BlockSpec((1, p.share, rows, p.wide), lambda i: (i, 0, 0, 0)),
            hbm(1)[0],
            whole(2, rows, LANES),
        ],
        out_shape=[
            jax.ShapeDtypeStruct((p.group, p.share, rows, p.wide), jnp.float32),
            pltpu.HBM((2 * p.half, rows, nlon), jnp.float32),
            jax.ShapeDtypeStruct((2, rows, LANES), jnp.float32),
        ],
        scratch_shapes=[
            pltpu.VMEM((2 * p.half, rows, nlon), jnp.float32),
            pltpu.VMEM((2 * p.half, rows, nlon), jnp.float32),
            pltpu.SemaphoreType.DMA(()),
        ],
        compiler_params=ROOM,
        cost_estimate=cost(p, 2),
        name="adjoint_second",
    )(perturb, weight, mine, other)


def cost(p, size):
    cells = p.members * p.fields * p.rows * p.nlon
    return pl.CostEstimate(flops=2 * cells, bytes_accessed=size * cells, transcendentals=0)


def forward_kernel(p, perturb, field, keep, send, held, scr, sem):
    cut = -(-p.vars // 2)
    parts = [(t, 0, p.vars) for t in range(p.slots - 1)]
    parts += [(p.slots - 1, 0, cut), (p.slots - 1, cut, p.vars)]
    moves = []
    for n, (t, low, high) in enumerate(parts):
        at = (slice(None), t, pl.ds(low, high - low))
        moves.append(pltpu.make_async_copy(perturb.at[at], held.at[at], sem.at[n]))
        moves[-1].start()

    one = jnp.zeros((1, 1), jnp.float32)
    two = jnp.zeros((1, 1), jnp.float32)
    for k in range(p.group):
        one = one + field[k * p.share, :1, p.nlon : p.nlon + 1]
        two = two + field[k * p.share, :1, p.nlon + SUB : p.nlon + SUB + 1]
    for k in range(2 * p.half):
        scr[k, :, p.nlon :] = jnp.zeros((p.rows, p.wide - p.nlon), jnp.float32)
    for k in (0, p.half):
        scr[k, :, p.nlon : p.nlon + SUB] = jnp.broadcast_to(one, (p.rows, SUB))
        scr[k, :, p.nlon + SUB : p.nlon + 2 * SUB] = jnp.broadcast_to(two, (p.rows, SUB))
    for k in range(p.fields, 2 * p.half):
        scr[k, :, : p.nlon] = jnp.zeros((p.rows, p.nlon), jnp.float32)

    split = p.nlon // (2 * LANES) * LANES
    for move, (t, low, high) in zip(moves, parts):
        move.wait()
        for cols in (slice(0, split), slice(split, p.nlon)):
            acc = [0.0] * (high - low)
            for m in range(p.members):
                f = field[m, :, cols]
                for v in range(low, high):
                    acc[v - low] += held[m, t, v, :, cols].astype(jnp.float32) * f
            for v in range(low, high):
                scr[t * p.vars + v, :, cols] = acc[v - low]

    core = lax.axis_index("mem") % 2
    for k in range(p.half):
        keep[k] = scr[core * p.half + k]
        send[k] = scr[(1 - core) * p.half + k]


def forward(p, perturb, field, hold):
    shape = (p.half, p.rows, p.wide)
    scratch = [
        pltpu.VMEM((2 * p.half, p.rows, p.wide), jnp.float32),
        pltpu.SemaphoreType.DMA((p.slots + 1,)),
    ]
    outs = [jax.ShapeDtypeStruct(shape, jnp.float32)] * 2
    if hold:
        outs = outs + [jax.ShapeDtypeStruct(perturb.shape, perturb.dtype)]
    else:
        scratch = [pltpu.VMEM(perturb.shape, perturb.dtype)] + scratch
    return pl.pallas_call(
        functools.partial(forward_kernel, p),
        in_specs=hbm(1) + vmem(1),
        out_specs=vmem(len(outs)),
        out_shape=outs,
        scratch_shapes=scratch,
        compiler_params=ROOM,
        cost_estimate=cost(p, 2),
        name="forward",
    )(pltpu.with_memory_space_constraint(perturb, pltpu.HBM), field)


def roll(x, shift, axis):
    return pltpu.roll(x, shift % x.shape[axis], axis)


def flip(p, pick, sheet):
    for j in range(p.wide // LANES):
        cols = slice(j * LANES, (j + 1) * LANES)
        tiles = [pick(c, m, cols) for m in range(p.share) for c in range(p.window)]
        if p.used < p.lanes:
            tiles.append(jnp.zeros((p.lanes - p.used, LANES), jnp.float32))
        block = jnp.concatenate(tiles, axis=0)
        for t in range(p.tiles):
            sheet[t, cols, :] = block[t * LANES : (t + 1) * LANES].T


def unflip(p, sheet, out, stop):
    for j in range(-(-stop // LANES)):
        low, high = j * LANES, min((j + 1) * LANES, stop)
        block = [sheet[t, low : low + LANES, :].T for t in range(p.tiles)]
        for m in range(p.share):
            for c in range(p.group):
                at = m * p.run + (p.halo + c) * p.rows
                piece = block[at // LANES][at % LANES : at % LANES + p.rows]
                out[c, m, :, low:high] = piece[:, : high - low]


def lane_row(p):
    lane = lax.broadcasted_iota(jnp.int32, (SUB, p.lanes), 1)
    return lane % p.run, lane


def wrap(p, buf):
    buf[0] = roll(buf[p.step], 1, 0)
    buf[p.step + 1] = roll(buf[1], -1, 0)


def tile(t):
    return slice(t * LANES, (t + 1) * LANES)


def sheet_to(p, sheet, buf):
    def one(i, none):
        for t in range(p.tiles):
            buf[i + 1, :, tile(t)] = sheet[t, pl.ds(i, SUB, stride=p.step), :]
        return none
    lax.fori_loop(0, p.step, one, 0, unroll=p.unroll)


def to_sheet(p, buf, sheet):
    def one(i, none):
        for t in range(p.tiles):
            sheet[t, pl.ds(i, SUB, stride=p.step), :] = buf[i + 1, :, tile(t)]
        return none
    lax.fori_loop(0, p.step, one, 0, unroll=p.unroll)


def one_pass(p, src, dst, east, north, south, diag):
    def body(c, carry):
        f, fw, west = carry
        for k in range(p.stride):
            i = 1 + c * p.stride + k
            fe, here = src[i + 1], east[i]
            across = north[i] * roll(f, -1, 1) + south[i] * roll(f, 1, 1)
            dst[i] = (diag[i] * f + across) + (here * fe + west * fw)
            f, fw, west = fe, f, here
        return f, fw, west
    lax.fori_loop(0, p.step // p.stride, body, (src[1], src[0], east[0]))
    wrap(p, dst)


def ten(p, a, b, *coefs):
    def two(_, none):
        one_pass(p, a, b, *coefs)
        one_pass(p, b, a, *coefs)
        return none
    lax.fori_loop(0, PASSES // 2, two, 0)
    if PASSES % 2:
        one_pass(p, a, b, *coefs)
        a[...] = b[...]


def put(p, sheet, i, value):
    for t in range(p.tiles):
        sheet[t, pl.ds(i, SUB, stride=p.step), :] = value[:, tile(t)]


def own_lanes(p):
    row, lane = lane_row(p)
    first = p.halo * p.rows
    return (row >= first) & (row < first + p.group * p.rows) & (lane < p.used)


def ends(p):
    if p.groups == 1:
        return 0, p.run - 1
    here = lax.axis_index("lat") // p.group * p.group - p.halo
    return jnp.maximum(-here, 0) * p.rows, jnp.minimum(p.lat - here, p.window) * p.rows - 1


def spread(p, low, high, inside, lower, east, north, south, diag):
    row, lane = lane_row(p)

    def coefs(i, none):
        below = lower[i + 1]
        if inside is not None:
            below = jnp.where(inside, below, 0.0)
            lower[i + 1] = below
        above = jnp.where(row < high, roll(below, -1, 1), 0.0)
        diag[i + 1] = (1.0 - (below + above)) - (east[i + 1] + east[i])
        north[i + 1] = above
        south[i + 1] = jnp.where(row > low, below, 0.0)
        return none
    lax.fori_loop(0, p.step, coefs, 0, unroll=p.unroll)


def first_kernel(p, got, near, far, out, *refs):
    stores, sheet, a, b, north, south, diag, right, east, lower, rows_right, coef, sem = (
        refs[:4], *refs[4:]
    )
    row, lane = lane_row(p)
    low, high = ends(p)
    mine = lax.axis_index("mem") % p.parts
    for k in range(max(p.parts // 2, 1)):
        coef[mine ^ k] = near[k]
    for k in range(p.parts // 2):
        coef[mine ^ (p.parts // 2) ^ k] = far[k]
    per = p.piece // LANES

    def pick(which):
        def of(c, m, cols):
            j = cols.start // LANES
            return coef[j // per, c, which, :, tile(j % per)]
        return of
    flip(p, pick(1), sheet)
    sheet_to(p, sheet, lower)
    flip(p, pick(0), sheet)
    sheet_to(p, sheet, east)
    wrap(p, east)
    inside = (row >= low) & (row <= high) & (lane < p.used)

    spread(p, low, high, inside, lower, east, north, south, diag)
    flip(p, lambda c, m, cols: got[c, m, :, cols], sheet)
    sheet_to(p, sheet, a)
    wrap(p, a)
    ten(p, a, b, east, north, south, diag)

    def keep(i, acc):
        b0 = a[i + 1]
        right[i + 1] = b0
        put(p, sheet, i, b0)
        return acc + b0 * b0
    rr = lax.fori_loop(0, p.step, keep, jnp.zeros((SUB, p.lanes), jnp.float32), unroll=p.unroll)
    rr = jnp.sum(jnp.where(own_lanes(p), rr, 0.0))
    unflip(p, sheet, rows_right, p.nlon)
    moves = [
        pltpu.make_async_copy(src, dst, sem.at[k])
        for k, (src, dst) in enumerate(zip((rows_right, right, east, lower), stores))
    ]
    for move in moves:
        move.start()
    ten(p, a, b, east, north, south, diag)
    to_sheet(p, a, sheet)
    sheet[:, p.nlon :, :] = jnp.full((p.tiles, p.wide - p.nlon, LANES), rr)
    unflip(p, sheet, out, p.wide)
    for move in moves:
        move.wait()


def second_kernel(p, got, scal, *refs):
    loads, out, store, ahead, sheet, a, b, north, south, diag, right, east, lower, rows_resid, sem = (
        refs[:3], *refs[3:]
    )
    row, lane = lane_row(p)
    moves = [
        pltpu.make_async_copy(src, dst, sem.at[k])
        for k, (src, dst) in enumerate(zip(loads, (east, lower, right)))
    ]
    for move in moves:
        move.start()
    flip(p, lambda c, m, cols: got[c, m, :, cols], sheet)
    if p.groups == 1:
        q = 0.0
        for t in range(p.tiles):
            first = (row[:1, tile(t)] % p.rows == 0) & (lane[:1, tile(t)] < p.run)
            q = q + jnp.sum(jnp.where(first, sheet[t, p.nlon : p.nlon + 1, :], 0.0))
        q = jnp.full((SUB, LANES), q)
    else:
        q = scal[1][:SUB]
    rr = scal[0][:SUB]
    alpha = rr / (rr + q)
    ahead[...] = alpha
    sheet_to(p, sheet, a)
    wrap(p, a)
    moves[0].wait()
    moves[1].wait()
    spread(p, *ends(p), None, lower, east, north, south, diag)
    ten(p, a, b, east, north, south, diag)
    moves[2].wait()
    alpha = jnp.broadcast_to(alpha[:, :1], (SUB, p.lanes))

    def cut(i, sums):
        r0 = right[i + 1]
        r = r0 - alpha * (r0 + a[i + 1])
        a[i + 1] = r
        put(p, sheet, i, r)
        return sums[0] + r * r, sums[1] + r * r0
    zero = jnp.zeros((SUB, p.lanes), jnp.float32)
    rr1, rb = lax.fori_loop(0, p.step, cut, (zero, zero), unroll=p.unroll)
    wrap(p, a)
    own = own_lanes(p)
    rr1 = jnp.sum(jnp.where(own, rr1, 0.0))
    rb = jnp.sum(jnp.where(own, rb, 0.0))
    unflip(p, sheet, rows_resid, p.nlon)
    leave = pltpu.make_async_copy(rows_resid, store, sem.at[3])
    leave.start()
    ten(p, a, b, east, north, south, diag)
    to_sheet(p, a, sheet)
    sheet[:, p.nlon :, :] = jnp.zeros((p.tiles, p.wide - p.nlon, LANES), jnp.float32)
    sheet[:, p.nlon : p.nlon + SUB, :] = jnp.full((p.tiles, SUB, LANES), rr1)
    sheet[:, p.nlon + SUB : p.nlon + 2 * SUB, :] = jnp.full((p.tiles, SUB, LANES), rb)
    unflip(p, sheet, out, p.wide)
    leave.wait()


def vmem(n):
    return [pl.BlockSpec(memory_space=pltpu.VMEM)] * n


def hbm(n):
    return [pl.BlockSpec(memory_space=pltpu.HBM)] * n


def half_shapes(p):
    buf = (p.step + 2, SUB, p.lanes)
    rows = (p.group, p.share, p.rows, p.nlon)
    back = (p.group, p.share, p.rows, p.wide)
    scratch = [pltpu.VMEM((p.tiles, p.wide, LANES), jnp.float32)]
    scratch += [pltpu.VMEM(buf, jnp.float32)] * 8
    scratch += [pltpu.VMEM(rows, jnp.float32)]
    return *(jax.ShapeDtypeStruct(x, jnp.float32) for x in (buf, rows, back)), scratch


def first_half(p, got, near, far):
    buf, rows, back, scratch = half_shapes(p)
    coef = pltpu.VMEM((p.parts, p.window, 2, p.rows, p.piece), jnp.float32)
    return pl.pallas_call(
        functools.partial(first_kernel, p),
        in_specs=vmem(3),
        out_specs=vmem(1) + hbm(4),
        out_shape=[back] + [pltpu.HBM(x.shape, x.dtype) for x in (rows, buf, buf, buf)],
        scratch_shapes=scratch + [coef, pltpu.SemaphoreType.DMA((4,))],
        compiler_params=ROOM,
        name="smooth_first",
    )(got, near, far)


def second_half(p, got, scal, right, east, lower):
    buf, rows, back, scratch = half_shapes(p)
    return pl.pallas_call(
        functools.partial(second_kernel, p),
        in_specs=vmem(2) + hbm(3),
        out_specs=vmem(1) + hbm(1) + vmem(1),
        out_shape=[
            back,
            pltpu.HBM(rows.shape, rows.dtype),
            jax.ShapeDtypeStruct((SUB, LANES), jnp.float32),
        ],
        scratch_shapes=scratch + [pltpu.SemaphoreType.DMA((4,))],
        compiler_params=ROOM,
        name="smooth_second",
    )(got, scal, *(pltpu.with_memory_space_constraint(x, pltpu.HBM) for x in (east, lower, right)))


def scalars(p, mine, scal):
    rr1 = mine[0, :1, p.nlon : p.nlon + 1]
    rb = mine[0, :1, p.nlon + SUB : p.nlon + SUB + 1]
    rr = scal[0][:1, :1]
    beta = rr1 / rr
    return rr1, beta, rr1 + beta * (2.0 * rb + beta * rr)


def test_kernel(p, weight, total, mine, scal, part, held, sem):
    at = lax.axis_index("mem") % 2 * p.half
    load = pltpu.make_async_copy(total.at[pl.ds(at, p.half)], held, sem)
    load.start()
    beta = scalars(p, mine, scal)[1]
    acc = jnp.zeros((p.rows, p.nlon), jnp.float32)
    load.wait()
    for k in range(p.half):
        t = mine[k, :, : p.nlon] + beta * held[k]
        acc = acc + weight[jnp.minimum(at + k, p.fields - 1)] * t * t
    acc = jnp.broadcast_to(jnp.sum(acc, axis=(0, 1), keepdims=True), part.shape[1:])
    for k in range(part.shape[0]):
        part[k] = acc


def test(p, weight, total, mine, scal):
    copies = 1 if p.groups > 1 else p.mem * p.lat
    return pl.pallas_call(
        functools.partial(test_kernel, p),
        in_specs=vmem(1) + hbm(1) + vmem(2),
        out_specs=vmem(1)[0],
        out_shape=jax.ShapeDtypeStruct((copies, SUB, LANES), jnp.float32),
        scratch_shapes=[
            pltpu.VMEM((p.half, p.rows, p.nlon), jnp.float32),
            pltpu.SemaphoreType.DMA(()),
        ],
        compiler_params=ROOM,
        name="last_sums",
    )(weight, pltpu.with_memory_space_constraint(total, pltpu.HBM), mine, scal)


def last_kernel(p, total, mine, other, scal, ahead, q, right, resid, grown, control, *refs):
    held, gbuf, cbuf, sem = refs
    load = pltpu.make_async_copy(total, held, sem.at[0])
    load.start()
    core = lax.axis_index("mem") % 2
    rr1, beta, length = scalars(p, mine, scal)
    every = q[0]
    for k in range(1, q.shape[0]):
        every = every + q[k]
    every = every[:1, :1] * (2.0 / p.mem)
    step1 = ahead[:1, :1]
    step2 = rr1 / (length + every)
    near = step1 + step2 * beta
    moves = []
    cuts = (0, p.members // 2, p.members)
    for n in range(2):
        for m in range(cuts[n], cuts[n + 1]):
            cbuf[m] = near * right[m] + step2 * resid[m]
        rows = pl.ds(cuts[n], cuts[n + 1] - cuts[n])
        moves.append(pltpu.make_async_copy(cbuf.at[rows], control.at[rows], sem.at[1 + n]))
        moves[-1].start()
    load.wait()
    for half, at in ((mine, core * p.half), (other, (1 - core) * p.half)):
        for k in range(p.half):
            gbuf[at + k] = near * held[at + k] + step2 * half[k, :, : p.nlon]
    moves.append(pltpu.make_async_copy(gbuf.at[pl.ds(0, p.fields)], grown, sem.at[3]))
    moves[-1].start()
    for move in moves:
        move.wait()


def last(p, total, mine, other, scal, ahead, q, right, resid):
    shape = (2 * p.half, p.rows, p.nlon)
    return pl.pallas_call(
        functools.partial(last_kernel, p),
        in_specs=hbm(1) + vmem(7),
        out_specs=hbm(2),
        out_shape=[
            pltpu.HBM((p.fields, p.rows, p.nlon), jnp.float32),
            pltpu.HBM((p.members, p.rows, p.nlon), jnp.float32),
        ],
        scratch_shapes=[
            pltpu.VMEM(shape, jnp.float32),
            pltpu.VMEM(shape, jnp.float32),
            pltpu.VMEM((p.members, p.rows, p.nlon), jnp.float32),
            pltpu.SemaphoreType.DMA((4,)),
        ],
        compiler_params=ROOM,
        name="last_update",
    )(
        pltpu.with_memory_space_constraint(total, pltpu.HBM),
        mine, other, scal, ahead, q, right, resid,
    )


def swap(p, x, axis, bit, count):
    return lax.ppermute(x, axis, [(i, i ^ bit) for i in range(count)])


def turn(p, x):
    if p.groups == 1:
        return lax.all_to_all(x, "lat", 0, 0)
    sets = [[g * p.group + i for i in range(p.group)] for g in range(p.groups)]
    return lax.all_to_all(x, "lat", 0, 0, axis_index_groups=sets)


def widen(p, x):
    if p.groups == 1:
        return x
    gap = p.group
    up = [(i, i + gap) for i in range(p.lat - gap)]
    down = [(i + gap, i) for i in range(p.lat - gap)]
    before = lax.ppermute(x[-p.halo :], "lat", up)
    after = lax.ppermute(x[: p.halo], "lat", down)
    return jnp.concatenate([before, x, after], axis=0)


def member_sum(p, keep, send):
    mine = keep + swap(p, send, "mem", 1, p.mem)
    bit = 2
    while bit < p.mem:
        mine = mine + swap(p, mine, "mem", bit, p.mem)
        bit *= 2
    if p.groups > 1:
        tail = lax.psum(mine[:1, :, p.nlon :], "lat") / p.group
        mine = lax.dynamic_update_slice(mine, tail, (0, 0, p.nlon))
    return mine


def coefficients(p, lon_coef, lat_coef):
    both = jnp.pad(jnp.stack([lon_coef, lat_coef]), ((0, 0), (0, 0), (0, p.wide - p.nlon)))
    part = lax.axis_index("mem") % p.parts
    both = lax.dynamic_slice_in_dim(both, part * p.piece, p.piece, axis=2)
    return turn(p, jnp.broadcast_to(both[None], (p.group, 2, p.rows, p.piece)))


def share_out(p, pieces):
    near = widen(p, pieces)[None]
    if p.parts == 1:
        return near, near
    if p.parts == 4:
        near = jnp.concatenate([near, swap(p, near, "mem", 1, p.mem)])
    return near, swap(p, near, "mem", p.parts // 2, p.mem)


def per_device(perturb, innovation, obs_weight, lon_coef, lat_coef):
    p = Plan(perturb, lat_coef, lax.axis_size("mem"), lax.axis_size("lat"))
    flat = lambda x: x.reshape(p.fields, p.rows, p.nlon)
    by_rank = lambda x: x.reshape((p.members,) + x.shape[2:])
    weight = flat(obs_weight)
    by_member = perturb.reshape(p.members, p.fields, p.rows, p.nlon)

    pieces = coefficients(p, lon_coef, lat_coef)
    sent = adjoint_first(p, by_member, weight, flat(innovation))
    near, far = share_out(p, pieces)
    back, rows_right, *kept = first_half(p, widen(p, turn(p, sent)), near, far)
    field, rows_right = lax.optimization_barrier((turn(p, back), rows_right))
    with jax.named_scope("return_first"):
        rows_right = by_rank(turn(p, rows_right))
    with jax.named_scope("map_first"):
        keep, send, held = forward(p, perturb, by_rank(field), True)
    mine = member_sum(p, keep, send)
    other = swap(p, mine, "mem", 1, p.mem)
    sent, total, scal = adjoint(p, held.reshape(by_member.shape), weight, mine, other)
    sent, rows_right = lax.optimization_barrier((sent, rows_right))
    if p.groups > 1:
        scal = jnp.concatenate([scal[:1], lax.psum(scal[1:], "lat")], axis=0)
    back, rows_resid, ahead = second_half(p, widen(p, turn(p, sent)), scal, *kept)
    field, rows_resid = lax.optimization_barrier((turn(p, back), rows_resid))
    with jax.named_scope("return_second"):
        rows_resid = by_rank(turn(p, rows_resid))
    with jax.named_scope("map_second"):
        keep, send = forward(p, perturb, by_rank(field), False)
    mine = member_sum(p, keep, send)
    mine, rows_resid = lax.optimization_barrier((mine, rows_resid))
    other = swap(p, mine, "mem", 1, p.mem)
    q = test(p, weight, total, mine, scal)
    q = lax.all_to_all(q, ("mem", "lat"), 0, 0) if p.groups == 1 else lax.psum(q, ("mem", "lat"))
    grown, control = last(p, total, mine, other, scal, ahead, q, rows_right, rows_resid)
    return control, grown.reshape(p.slots, p.vars, p.rows, p.nlon)


def solution(mesh):
    return jax.shard_map(
        per_device,
        mesh=mesh,
        in_specs=(
            P("mem", None, None, "lat", None),
            P(None, None, "lat", None),
            P(None, None, "lat", None),
            P("lat", None),
            P("lat", None),
        ),
        out_specs=(P("mem", "lat", None), P(None, None, "lat", None)),
        check_vma=False,
    )
```
